512 devices in a mesh: round: 128 (over z, y, core), mp: 4 (over x).
Axes of the slice: x: 4, y: 8, z: 8, core: 2. Of those that a mesh axis runs over, the one named last changes fastest.
Arguments:
- tokens: bfloat16 [128, 512, 512], P('round'), may hold values from -8 to 8
- cell_order: int32 [512], replicated, may hold values from 0 to 511, each once
- seam_rows: int32 [128, 128, 2], P('round'), may hold values from -1 to 511, as said below
- obs_mask: int32 [16, 512], replicated, may hold values from 0 to 1, as said below
- norm_gain: float32 [512], replicated, may hold values from 0.1 to 1.9
- w_query: bfloat16 [512, 512], P(None, 'mp'), may hold values from -1 to 1
- w_key: bfloat16 [512, 512], P(None, 'mp'), may hold values from -1 to 1
- w_value: bfloat16 [512, 512], P(None, 'mp'), may hold values from -0.25 to 0.25
- w_out: bfloat16 [512, 512], P('mp'), may hold values from -0.25 to 0.25
- w_gate: bfloat16 [512, 2048], P(None, 'mp'), may hold values from -0.25 to 0.25
- w_up: bfloat16 [512, 2048], P(None, 'mp'), may hold values from -0.25 to 0.25
- w_down: bfloat16 [2048, 512], P('mp'), may hold values from -0.125 to 0.125
- w_read: float32 [512], replicated, may hold values from -0.25 to 0.25
Outputs:
- tiles_out: bfloat16 [128, 512, 512], P('mp', 'round')
- obs_logits: float32 [16], replicated
The draws below stay inside these ranges and needn't reach their ends.
Inputs may be any that keep to these rules, and one draw needn't show every extreme that they name: `seam_rows`: each entry is a row of the sending tile or -1 for an empty slot; the live entries of one tile are all different; a tile's slots to itself are full, and some owner's slots are full from every tile. `obs_mask`: every observable's support holds at least one cell.
All inputs are finite; a program needn't handle non-finite values.
Results may differ from the reference program's by a relative error of at most 0.0052.
The reference program's roundings to bfloat16 on the way (of `permuted`, `normed`, `seam_attn`, `combined` and `hidden`) count: a program that leaves them out, or rounds other values in their place, can miss the bound.
Values may be sent and summed in bfloat16 or wider, within the bound.
A program may use at most 64 MiB of HBM per device.

```python
import math
import jax
import jax.numpy as jnp
from jax import lax

D = 512
HEADS = 8
HDIM = 64
FF = 2048
OBS = 16
CAP = 2
CELL_DEV = 4
ROUNDS = 128
OWNERS = 128
CELLS = 512
TILE_ROWS = 512


def draw_tokens(key, part):
    shape_all = (ROUNDS, CELLS, D)
    drawn = jnp.clip(jax.random.normal(jax.random.fold_in(key, 1), shape_all, jnp.float32), -6.0, 6.0)
    return drawn.astype(jnp.bfloat16)


def projection(key, salt):
    base = jax.random.normal(jax.random.fold_in(key, salt), (D, D), jnp.float32) / math.sqrt(D)
    base = jnp.clip(base, -0.5, 0.5)
    return base.astype(jnp.bfloat16)


def draw_w_query(key, part):
    return projection(key, 21)


def draw_w_key(key, part):
    return projection(key, 22)


def draw_seam_rows(key, part):
    light_load = jax.random.randint(jax.random.fold_in(key, 31), (OWNERS, OWNERS), 0, CAP + 1)
    heavy_owner = jax.random.randint(jax.random.fold_in(key, 32), (OWNERS,), 0, 8) == 0
    hottest = jax.random.randint(jax.random.fold_in(key, 33), (), 0, OWNERS)
    owners_list = jnp.arange(OWNERS, dtype=jnp.int32)
    filled = heavy_owner[None, :] | (owners_list[None, :] == hottest) | (owners_list[None, :] == owners_list[:, None])
    counts = jnp.where(filled, CAP, light_load)

    def sender_rows(sender):
        shuffled = jax.random.permutation(jax.random.fold_in(jax.random.fold_in(key, 34), sender), TILE_ROWS).astype(jnp.int32)
        where_top = jnp.argmax(shuffled == TILE_ROWS - 1)
        anchor = sender * CAP
        moved_value = shuffled[anchor]
        shuffled = shuffled.at[where_top].set(moved_value).at[anchor].set(TILE_ROWS - 1)
        return shuffled[:OWNERS * CAP].reshape(OWNERS, CAP)
    picked_rows = jax.vmap(sender_rows)(owners_list)
    slot_index = jnp.arange(CAP, dtype=jnp.int32)
    return jnp.where(slot_index[None, None, :] < counts[:, :, None], picked_rows, -1).astype(jnp.int32)


def draw_obs_mask(key, part):
    level = jax.random.randint(jax.random.fold_in(key, 41), (OBS, 1), 8, 33)
    rolls = jax.random.randint(jax.random.fold_in(key, 42), (OBS, CELLS), 0, 64)
    anchor = jax.random.randint(jax.random.fold_in(key, 43), (OBS, 1), 0, CELLS)
    cell_index = jnp.arange(CELLS, dtype=jnp.int32)[None, :]
    return ((rolls < level) | (cell_index == anchor)).astype(jnp.int32)


def block_levels(key, extent, shards, least, high):
    loudness, own = 1.0, jax.random.fold_in(key, 6)
    for position, parts in shards:
        steps = jnp.exp(jax.random.uniform(jax.random.fold_in(own, position), (parts,), jnp.float32, least / len(shards), high / len(shards)))
        loudness = loudness * jnp.repeat(steps, extent[position] // parts).reshape([-1 if axis == position else 1 for axis in range(len(extent))])
    return loudness


def scatter_about(rng, dims, width, limit, cuts=(), held_as=jnp.bfloat16):
    loudness = block_levels(rng, dims, cuts, -0.22, 0.18) if cuts else 1.0
    values = jax.random.normal(rng, dims, jnp.float32) * width * loudness
    return jnp.minimum(jnp.maximum(values, -limit), limit).astype(held_as)


def setup_inputs(seed: int = 0) -> dict:
    arg_keys = jax.random.split(jax.random.key(seed), 14)
    tokens = draw_tokens(jax.random.fold_in(arg_keys[13], 71), 0)
    cell_order = jax.random.permutation(arg_keys[1], CELLS).astype(jnp.int32)
    seam_rows = draw_seam_rows(jax.random.fold_in(arg_keys[13], 71), 0)
    obs_mask = draw_obs_mask(jax.random.fold_in(arg_keys[13], 71), 0)
    norm_gain = jnp.clip(1.0 + 0.18 * jax.random.normal(arg_keys[4], (D,), jnp.float32), 0.1, 1.9)
    w_query = draw_w_query(jax.random.fold_in(arg_keys[13], 71), 0)
    w_key = draw_w_key(jax.random.fold_in(arg_keys[13], 71), 0)
    w_value = scatter_about(arg_keys[7], (D, D), D ** -0.5, 0.25, ((1, 4),))
    w_out = scatter_about(arg_keys[8], (D, D), D ** -0.5, 0.25, ((0, 4),))
    w_gate = scatter_about(arg_keys[9], (D, FF), D ** -0.5, 0.25, ((1, 4),))
    w_up = scatter_about(arg_keys[10], (D, FF), D ** -0.5, 0.25, ((1, 4),))
    w_down = scatter_about(arg_keys[11], (FF, D), FF ** -0.5, 0.125, ((0, 4),))
    w_read = scatter_about(arg_keys[12], (D,), D ** -0.5, 0.25, (), jnp.float32)
    return dict(tokens=tokens, cell_order=cell_order, seam_rows=seam_rows, obs_mask=obs_mask, norm_gain=norm_gain, w_query=w_query, w_key=w_key, w_value=w_value, w_out=w_out, w_gate=w_gate, w_up=w_up, w_down=w_down, w_read=w_read)


norm_eps = 1e-06

def normalize(rows_in, norm_gain):
    values = rows_in.astype(jnp.float32)
    spread = lax.optimization_barrier(jnp.mean(values * values, axis=-1, keepdims=True))
    return (values * lax.rsqrt(spread + norm_eps) * norm_gain).astype(jnp.bfloat16)

def attend(queries, keys_all, values_all, live_keys):
    scale_factor = 1.0 / math.sqrt(queries.shape[-1])
    scores = jnp.einsum('qhe,khe->hqk', queries.astype(jnp.float32), keys_all.astype(jnp.float32)) * scale_factor
    if live_keys is not None:
        scores = jnp.where(live_keys[None, None, :], scores, -1e+30)
    row_max = lax.optimization_barrier(jnp.max(scores, axis=-1, keepdims=True))
    weights = jnp.exp(scores - row_max)
    probabilities = (weights / lax.optimization_barrier(jnp.sum(weights, axis=-1, keepdims=True))).astype(jnp.bfloat16)
    mixture = jnp.einsum('hqk,khe->qhe', probabilities.astype(jnp.float32), values_all.astype(jnp.float32))
    return mixture.reshape(mixture.shape[0], -1)

def reference(tokens, cell_order, seam_rows, obs_mask, norm_gain, w_query, w_key, w_value, w_out, w_gate, w_up, w_down, w_read):
    permuted = tokens[:, cell_order, :]
    tile_tokens = permuted.reshape(ROUNDS, OWNERS, CELL_DEV, D).transpose(1, 0, 2, 3).reshape(OWNERS, TILE_ROWS, D)

    def to_heads(matrix):
        return matrix.reshape(matrix.shape[0], HEADS, HDIM)

    def project(tile_in):
        normed = normalize(tile_in, norm_gain)
        queries = jnp.dot(normed, w_query, preferred_element_type=jnp.float32).astype(jnp.bfloat16)
        keys_all = jnp.dot(normed, w_key, preferred_element_type=jnp.float32).astype(jnp.bfloat16)
        values_all = jnp.dot(normed, w_value, preferred_element_type=jnp.float32).astype(jnp.bfloat16)
        local_attn = attend(to_heads(queries), to_heads(keys_all), to_heads(values_all), None)
        return (normed, queries, keys_all, values_all, local_attn)
    normed, queries, keys_all, values_all, local_attn = lax.map(project, tile_tokens)
    live_slot = seam_rows >= 0
    safe_rows = jnp.where(live_slot, seam_rows, 0).astype(jnp.int32)
    senders = jnp.arange(OWNERS, dtype=jnp.int32)[:, None]

    def owner_attend(owner_index):
        picked = lax.dynamic_index_in_dim(safe_rows, owner_index, 1, keepdims=False)
        live_owner = lax.dynamic_index_in_dim(live_slot, owner_index, 1, keepdims=False).reshape(-1)
        gathered = [source[senders, picked].reshape(OWNERS * CAP, HEADS, HDIM) for source in (queries, keys_all, values_all)]
        return attend(gathered[0], gathered[1], gathered[2], live_owner).astype(jnp.bfloat16)
    seam_attn = lax.map(owner_attend, jnp.arange(OWNERS, dtype=jnp.int32))
    returned = seam_attn.reshape(OWNERS, OWNERS, CAP, D).transpose(1, 0, 2, 3).reshape(OWNERS, OWNERS * CAP, D)
    target = jnp.where(live_slot, seam_rows, TILE_ROWS).astype(jnp.int32).reshape(OWNERS, OWNERS * CAP)
    combined = local_attn.at[senders, target].add(returned.astype(jnp.float32), mode='drop').astype(jnp.bfloat16)

    def finish(pieces):
        tile_in, normed_in, combined_in = pieces
        attn_part = jnp.dot(combined_in, w_out, preferred_element_type=jnp.float32)
        gate_part = jnp.dot(normed_in, w_gate, preferred_element_type=jnp.float32)
        up_part = jnp.dot(normed_in, w_up, preferred_element_type=jnp.float32)
        hidden = (jax.nn.silu(gate_part) * up_part).astype(jnp.bfloat16)
        update = attn_part + jnp.dot(hidden, w_down, preferred_element_type=jnp.float32)
        return (tile_in.astype(jnp.float32) + update).astype(jnp.bfloat16)
    tiles_done = lax.map(finish, (tile_tokens, normed, combined))
    layout = tiles_done.reshape(OWNERS, ROUNDS, CELL_DEV, D).transpose(1, 0, 2, 3).reshape(ROUNDS, CELLS, D)
    support = obs_mask[:, cell_order].astype(jnp.float32)
    pooled = jnp.einsum('oc,rcd->od', support, layout.astype(jnp.float32), precision=lax.Precision.HIGHEST)
    support_count = ROUNDS * lax.optimization_barrier(jnp.sum(obs_mask.astype(jnp.float32), axis=1))
    obs_logits = jnp.dot(pooled, w_read, precision=lax.Precision.HIGHEST) / jnp.sqrt(support_count)
    return (layout, obs_logits)
```

```python
import jax
import jax.numpy as jnp
from jax import lax
from jax.experimental import pallas as pl
from jax.experimental.pallas import tpu as pltpu
from jax.sharding import PartitionSpec as P

F32 = jnp.float32
BF16 = jnp.bfloat16
MESH = pl.DeviceIdType.MESH
EPS = 1e-6
NZ, NYK, NX = 8, 16, 4
D, HD, ROWS = 512, 128, 512
MARK = 2.0 ** 100
DEAD = -1e30


def iota(shape, axis):
    return lax.broadcasted_iota(jnp.int32, shape, axis)


def hot(mask):
    return jnp.where(mask, 1.0, 0.0).astype(BF16)


def mm(a, b):
    return jnp.dot(a, b, preferred_element_type=F32)


def mm_nt(a, b):
    return lax.dot_general(a, b, (((1,), (1,)), ((), ())), preferred_element_type=F32)


def softmax(scores):
    top = jnp.max(scores, axis=-1, keepdims=True)
    weights = jnp.exp((scores - top) * 0.125)
    total = jnp.sum(weights, axis=-1, keepdims=True)
    return (weights * (1.0 / total)).astype(BF16)


def kernel(
    tokens, cells, seam, obs, gain, w_q, w_k, w_v, w_o, w_g, w_u, w_d, w_r,
    out, logits,
    wqkv, wo, wg, wu, wd,
    x1, b1, x2, tok, normed, normed_c, qkv, q_c, local,
    sx1, sb1, sx2, sb2, ra, rb1, rx, rb2,
    hot_t, ff, ffb, cx, cb, px, pz, py,
    w_sem, wo_send, wo_recv, s_send, s_recv, y_send, y_recv, x_send, x_recv,
    f_send, f_recv,
):
    me = lax.axis_index("round")
    m = lax.axis_index("mp")
    z = me // NYK
    yk = lax.rem(me, NYK)

    def at_z(i):
        return (i * NYK + yk, m)

    def at_yk(i):
        return (z * NYK + i, m)

    def at_x(i):
        return (me, i)

    def peer(kind, k):
        if kind == "z":
            i = lax.rem(z + k, NZ)
            return i, at_z(i)
        if kind == "y":
            i = lax.rem(yk + k, NYK)
            return i, at_yk(i)
        i = lax.rem(m + k, NX)
        return i, at_x(i)

    counts = {"z": NZ, "y": NYK, "x": NX}

    barrier = pltpu.get_barrier_semaphore()
    for kind in ("z", "y", "x"):
        for k in range(1, counts[kind]):
            pl.semaphore_signal(
                barrier, inc=1, device_id=peer(kind, k)[1], device_id_type=MESH
            )

    loads = [
        pltpu.make_async_copy(w_q, wqkv.at[:, pl.ds(0, HD)], w_sem.at[0]),
        pltpu.make_async_copy(w_k, wqkv.at[:, pl.ds(HD, HD)], w_sem.at[1]),
        pltpu.make_async_copy(w_v, wqkv.at[:, pl.ds(2 * HD, HD)], w_sem.at[2]),
        pltpu.make_async_copy(w_g, wg, w_sem.at[3]),
        pltpu.make_async_copy(w_u, wu, w_sem.at[4]),
        pltpu.make_async_copy(w_d, wd, w_sem.at[5]),
        pltpu.make_async_copy(w_o, wo.at[m], w_sem.at[6]),
    ]
    for load in loads:
        load.start()

    def exchange(kind, src, dst, send, recv):
        started = []
        for k in range(1, counts[kind]):
            i, where = peer(kind, k)
            copy = pltpu.make_async_remote_copy(
                src_ref=src(i),
                dst_ref=dst,
                send_sem=send.at[k],
                recv_sem=recv.at[k],
                device_id=where,
                device_id_type=MESH,
            )
            copy.start()
            started.append(copy)
        return started

    def finish(started):
        for copy in started:
            copy.wait()

    cell_row = cells[...].astype(F32)
    pick = iota((128, 512), 1) == 4 * iota((128, 512), 0) + m
    cell_col = jnp.sum(jnp.where(pick, cell_row, 0.0), axis=1, keepdims=True)
    lanes_f = iota((128, 512), 1).astype(F32)
    x1[...] = mm(hot(lanes_f == cell_col), tokens[...]).astype(BF16).reshape(NZ, NYK, D)

    pl.semaphore_wait(barrier, (NZ - 1) + (NYK - 1) + (NX - 1))
    stage_z = exchange("z", lambda i: x1.at[i], b1.at[z], s_send.at[0], s_recv.at[0])
    loads[6].wait()
    share_wo = exchange("x", lambda i: wo.at[m], wo.at[m], wo_send, wo_recv)
    b1[z] = x1[z]

    own_pick = iota((128, 512), 1) == 4 * me + (iota((128, 512), 0) & 3)
    own_col = jnp.sum(jnp.where(own_pick, cell_row, 0.0), axis=1, keepdims=True)
    obs_all = jnp.concatenate(
        [obs[...].astype(F32), jnp.zeros((112, 512), F32)], axis=0
    ).astype(BF16)
    support = mm_nt(hot(lanes_f == own_col), obs_all)
    divisor = jnp.sqrt(128.0 * mm_nt(jnp.ones((8, 512), BF16), obs_all))[0:1]

    rows = seam[...]
    shuffled = (rows & 3) * 128 + ((rows >> 2) & 15) * 8 + (rows >> 6)
    shuffled = jnp.where(rows < 0, -1, shuffled)
    hot_g = jnp.concatenate(
        [hot(iota((128, 512), 1) == shuffled[:, c : c + 1]) for c in range(2)], axis=0
    )
    hot_c = jnp.concatenate(
        [hot(iota((128, 512), 1) == rows[:, c : c + 1]) for c in range(2)], axis=0
    )
    empty = jnp.concatenate([rows[:, c : c + 1] < 0 for c in range(2)], axis=0)
    hot_t[...] = hot_c.astype(F32).T.astype(BF16)

    q, p = iota((128, 128), 0), iota((128, 128), 1)
    turn = hot(p == (q & 7) * NYK + (q >> 3))
    finish(stage_z)
    x2[...] = mm(turn, b1[...].reshape(128, D)).astype(BF16).reshape(NYK, NZ, D)
    mine = tok.at[m]
    stage_y = exchange("y", lambda i: x2.at[i], mine.at[yk], y_send.at[0], y_recv.at[0])
    tok[m, yk] = x2[yk]
    for load in loads[:3]:
        load.wait()
    finish(stage_y)

    stage_x = exchange("x", lambda i: tok.at[m], tok.at[m], x_send.at[0], x_recv.at[0])
    gain_row = gain[...]
    finish(stage_x)

    def norm_step(c, carry):
        values = tok[c].reshape(128, D).astype(F32)
        spread = jnp.mean(values * values, axis=-1, keepdims=True)
        normal = (values * lax.rsqrt(spread + EPS) * gain_row).astype(BF16)
        at = pl.ds(pl.multiple_of(c * 128, 128), 128)
        normed[at, :] = normal
        qkv[at, :] = mm(normal, wqkv[...]).astype(BF16)
        return carry

    lax.fori_loop(0, 4, norm_step, 0)

    sent = mm(hot_g, qkv[...])
    lane = iota((256, 384), 1)
    sent = jnp.where((lane == 0) & empty, MARK, sent).astype(BF16)
    sx1[...] = sent.reshape(2, NZ, NYK, 3 * HD)
    seam_z = exchange("z", lambda i: sx1.at[:, i], sb1.at[z], s_send.at[1], s_recv.at[1])
    sb1[z] = sx1[:, z]

    a, b = iota((512, 512), 0), iota((512, 512), 1)
    natural = hot(b == (a & 3) * 128 + ((a >> 2) & 15) * 8 + (a >> 6))
    normed_c[...] = mm(natural, normed[...]).astype(BF16)
    q_c[...] = mm(natural, qkv[:, 0:HD]).astype(BF16)
    loads[3].wait()
    loads[4].wait()
    loads[5].wait()

    def ff_step(i, carry):
        at = pl.ds(pl.multiple_of(i * 128, 128), 128)
        block = normed_c[at, :]
        gate = mm(block, wg[...])
        up = mm(block, wu[...])
        hidden = (gate * (1.0 / (1.0 + jnp.exp(-gate))) * up).astype(BF16)
        ff[i] = mm(hidden, wd[...])
        return carry

    lax.fori_loop(0, 4, ff_step, 0)
    share_ff = exchange("x", lambda i: ff.at[i], ffb.at[m], f_send, f_recv)

    q2, p2 = iota((256, 256), 0), iota((256, 256), 1)
    turn_out = hot(p2 == (q2 & 7) * 32 + ((q2 >> 3) & 1) * 16 + (q2 >> 4))
    finish(seam_z)
    sx2[...] = mm(turn_out, sb1[...].reshape(256, 3 * HD)).astype(BF16).reshape(NYK, 16, 3 * HD)
    seam_y = exchange("y", lambda i: sx2.at[i], sb2.at[yk], y_send.at[1], y_recv.at[1])
    sb2[yk] = sx2[yk]
    ffb[m] = ff[m]

    low = iota((512, HD), 1) < 64
    for h in range(2):
        half = low if h == 0 else jnp.logical_not(low)
        keys = jnp.where(half, qkv[:, HD : 2 * HD], 0.0).astype(BF16)
        values = jnp.where(half, qkv[:, 2 * HD : 3 * HD], 0.0).astype(BF16)
        for blk in range(2):
            at = slice(blk * 256, blk * 256 + 256)
            weights = softmax(mm_nt(q_c[at, :], keys))
            mix = mm(weights, values)
            if h == 0:
                local[at, :] = mix
            else:
                local[at, :] += mix

    finish(seam_y)
    held = sb2[...].reshape(256, 3 * HD)
    sq, sk, sv = held[:, 0:HD], held[:, HD : 2 * HD], held[:, 2 * HD :]
    dead = sq[:, 0:1].astype(F32) > 1e20
    lane2 = iota((256, HD), 1)
    low2 = lane2 < 64
    total = jnp.zeros((256, HD), F32)
    sq = jnp.where(dead, 0.0, sq.astype(F32))
    skf, svf = sk.astype(F32), sv.astype(F32)
    for h in range(2):
        half = low2 if h == 0 else jnp.logical_not(low2)
        spot = lane2 == (64 if h == 0 else 0)
        queries = jnp.where(half, sq, jnp.where(spot, 1.0, 0.0)).astype(BF16)
        keys = jnp.where(half, skf, jnp.where(spot & dead, DEAD, 0.0)).astype(BF16)
        values = jnp.where(half, svf, 0.0).astype(BF16)
        total += mm(softmax(mm_nt(queries, keys)), values)
    ra[...] = total.astype(BF16).reshape(NYK, 16, HD)
    back_y = exchange("y", lambda i: ra.at[i], rb1.at[yk], y_send.at[2], y_recv.at[2])
    rb1[yk] = ra[yk]

    a2, b2 = iota((128, 512), 0) + 128 * m, iota((128, 512), 1)
    own = hot(b2 == (a2 & 3) * 128 + ((a2 >> 2) & 15) * 8 + (a2 >> 6))
    own_tok = mm(own, tok[...].reshape(ROWS, D))

    turn_back = hot(p2 == (q2 & 15) * 16 + ((q2 >> 4) & 1) * 8 + (q2 >> 5))
    finish(back_y)
    rx[...] = mm(turn_back, rb1[...].reshape(256, HD)).astype(BF16).reshape(NZ, 2, NYK, HD)
    back_z = exchange("z", lambda i: rx.at[i], rb2.at[:, z], s_send.at[2], s_recv.at[2])
    rb2[:, z] = rx[z]
    finish(share_wo)
    finish(share_ff)
    ff_own = ffb[0] + ffb[1] + ffb[2] + ffb[3]
    finish(back_z)

    both = local[...] + mm(hot_t[...], rb2[...].reshape(256, HD))
    cx[...] = both.astype(BF16).reshape(NX, 128, HD)
    comb_x = exchange("x", lambda i: cx.at[i], cb.at[m], x_send.at[1], x_recv.at[1])
    cb[m] = cx[m]
    finish(comb_x)
    attn = mm(cb[0], wo[0]) + mm(cb[1], wo[1]) + mm(cb[2], wo[2]) + mm(cb[3], wo[3])
    result = (own_tok + (attn + ff_own)).astype(BF16)
    out[...] = result

    dots = jnp.sum(result.astype(F32) * w_r[...], axis=1, keepdims=True)
    px[m] = jnp.sum(support * dots, axis=0, keepdims=True)
    sum_x = exchange("x", lambda i: px.at[m], px.at[m], x_send.at[2], x_recv.at[2])
    finish(sum_x)
    pz[z] = jnp.sum(px[...], axis=0)
    sum_z = exchange("z", lambda i: pz.at[z], pz.at[z], s_send.at[3], s_recv.at[3])
    finish(sum_z)
    py[yk] = jnp.sum(pz[...], axis=0)
    sum_y = exchange("y", lambda i: py.at[yk], py.at[yk], y_send.at[3], y_recv.at[3])
    finish(sum_y)
    pooled = jnp.sum(py[...], axis=0)
    logits[...] = (pooled / divisor)[:, 0:16]


def shards(
    tokens, cell_order, seam_rows, obs_mask, norm_gain,
    w_query, w_key, w_value, w_out, w_gate, w_up, w_down, w_read,
):
    vmem = pl.BlockSpec(memory_space=pltpu.VMEM)
    hbm = pl.BlockSpec(memory_space=pl.ANY)
    dma = pltpu.SemaphoreType.DMA
    V = pltpu.VMEM
    out, logits = pl.pallas_call(
        kernel,
        out_shape=(
            jax.ShapeDtypeStruct((128, D), BF16),
            jax.ShapeDtypeStruct((1, 16), F32),
        ),
        in_specs=[vmem] * 5 + [hbm] * 7 + [vmem],
        out_specs=(vmem, vmem),
        scratch_shapes=[
            V((D, 3 * HD), BF16), V((NX, HD, D), BF16), V((D, D), BF16),
            V((D, D), BF16), V((D, D), BF16),
            V((NZ, NYK, D), BF16), V((NZ, NYK, D), BF16), V((NYK, NZ, D), BF16),
            V((NX, NYK, NZ, D), BF16), V((ROWS, D), BF16), V((ROWS, D), BF16),
            V((ROWS, 3 * HD), BF16), V((ROWS, HD), BF16), V((ROWS, HD), F32),
            V((2, NZ, NYK, 3 * HD), BF16), V((NZ, 2, NYK, 3 * HD), BF16),
            V((NYK, 16, 3 * HD), BF16), V((NYK, 16, 3 * HD), BF16),
            V((NYK, 16, HD), BF16), V((NYK, 16, HD), BF16),
            V((NZ, 2, NYK, HD), BF16), V((2, NZ, NYK, HD), BF16),
            V((ROWS, 256), BF16), V((NX, 128, D), F32), V((NX, 128, D), F32),
            V((NX, 128, HD), BF16), V((NX, 128, HD), BF16),
            V((NX, 1, 128), F32), V((NZ, 1, 128), F32), V((NYK, 1, 128), F32),
            dma((7,)), dma((NX,)), dma((NX,)),
            dma((4, NZ)), dma((4, NZ)), dma((4, NYK)), dma((4, NYK)),
            dma((3, NX)), dma((3, NX)), dma((NX,)), dma((NX,)),
        ],
        compiler_params=pltpu.CompilerParams(
            collective_id=0, has_side_effects=True, vmem_limit_bytes=40 * 2 ** 20
        ),
    )(
        tokens.reshape(512, D), cell_order.reshape(1, 512), seam_rows.reshape(128, 2),
        obs_mask, norm_gain.reshape(1, D), w_query, w_key, w_value, w_out, w_gate,
        w_up, w_down, w_read.reshape(1, D),
    )
    return out.reshape(32, 4, D), logits.reshape(16)


def solution(mesh):
    return jax.shard_map(
        shards,
        mesh=mesh,
        in_specs=(
            P("round", None, None),
            P(),
            P("round", None, None),
            P(),
            P(),
            P(None, "mp"),
            P(None, "mp"),
            P(None, "mp"),
            P("mp", None),
            P(None, "mp"),
            P(None, "mp"),
            P("mp", None),
            P(),
        ),
        out_specs=(P("mp", "round", None), P()),
        check_vma=False,
    )
```

```python
import jax
import jax.numpy as jnp
from jax import lax
from jax.experimental import pallas as pl
from jax.experimental.pallas import tpu as pltpu
from jax.sharding import PartitionSpec as P

F32 = jnp.float32
BF16 = jnp.bfloat16
MESH = pl.DeviceIdType.MESH
EPS = 1e-6
ROUNDS, NX = 128, 4
D, HD, ROWS, SLOTS = 512, 128, 512, 256
MARK = 2.0 ** 100
DEAD = -1e30


def iota(shape, axis):
    return lax.broadcasted_iota(jnp.int32, shape, axis)


def hot(mask):
    return jnp.where(mask, 1.0, 0.0).astype(BF16)


def mm(a, b):
    return jnp.dot(a, b, preferred_element_type=F32)


def mm_nt(a, b):
    return lax.dot_general(a, b, (((1,), (1,)), ((), ())), preferred_element_type=F32)


def softmax(scores):
    top = jnp.max(scores, axis=-1, keepdims=True)
    weights = jnp.exp((scores - top) * 0.125)
    total = jnp.sum(weights, axis=-1, keepdims=True)
    return (weights * (1.0 / total)).astype(BF16)


def kernel(
    tokens_hbm, cells, seam, obs, gain, w_q, w_k, w_v, w_o, w_g, w_u, w_d, w_r,
    out, logits,
    tokens, wqkv, wo, wg, wu, wd,
    x1, tok, normed, qkv, local, sx, sb, ra, rb, hot_t, ff, ffb, cx, cb, px, pr,
    w_sem, r_send, r_recv, x_send, x_recv,
):
    me = lax.axis_index("round")
    m = lax.axis_index("mp")
    z, y, core = me // 16, lax.rem(me // 2, 8), lax.rem(me, 2)

    def far_first(k):
        return 4 + (1 - 2 * lax.rem(k, 2)) * ((k + 1) // 2)

    def round_peer(k):
        to_z = lax.rem(z + far_first(k // 16), 8)
        to_y = lax.rem(y + far_first(lax.rem(k // 2, 8)), 8)
        to_core = lax.rem(core + 1 - lax.rem(k, 2), 2)
        return to_z * 16 + to_y * 2 + to_core

    def x_peer(k):
        return lax.rem(m + k, NX)

    def send_rounds(src, dst, slot):
        def step(k, carry):
            to = round_peer(k)
            pltpu.make_async_remote_copy(
                src_ref=src(to),
                dst_ref=dst.at[me],
                send_sem=r_send.at[slot],
                recv_sem=r_recv.at[slot],
                device_id=(to, m),
                device_id_type=MESH,
            ).start()
            return carry

        lax.fori_loop(0, ROUNDS - 1, step, 0)

    def wait_rounds(buffer, sem, slot):
        others = buffer.at[pl.ds(0, ROUNDS - 1)]
        pltpu.make_async_copy(others, others, sem.at[slot]).wait()

    def send_x(src, dst, slot):
        started = []
        for k in (2, 1, 3):
            to = x_peer(k)
            copy = pltpu.make_async_remote_copy(
                src_ref=src(to),
                dst_ref=dst,
                send_sem=x_send.at[slot, k],
                recv_sem=x_recv.at[slot, k],
                device_id=(me, to),
                device_id_type=MESH,
            )
            copy.start()
            started.append(copy)
        return started

    def finish(started):
        for copy in started:
            copy.wait()

    load_tokens = pltpu.make_async_copy(tokens_hbm, tokens, w_sem.at[7])
    load_tokens.start()
    barrier = pltpu.get_barrier_semaphore()

    def greet(k, carry):
        pl.semaphore_signal(
            barrier, inc=1, device_id=(round_peer(k), m), device_id_type=MESH
        )
        return carry

    lax.fori_loop(0, ROUNDS - 1, greet, 0)
    for k in range(1, NX):
        pl.semaphore_signal(
            barrier, inc=1, device_id=(me, x_peer(k)), device_id_type=MESH
        )

    loads = [
        pltpu.make_async_copy(w_q, wqkv.at[:, pl.ds(0, HD)], w_sem.at[0]),
        pltpu.make_async_copy(w_k, wqkv.at[:, pl.ds(HD, HD)], w_sem.at[1]),
        pltpu.make_async_copy(w_v, wqkv.at[:, pl.ds(2 * HD, HD)], w_sem.at[2]),
        pltpu.make_async_copy(w_g, wg, w_sem.at[3]),
        pltpu.make_async_copy(w_u, wu, w_sem.at[4]),
        pltpu.make_async_copy(w_d, wd, w_sem.at[5]),
        pltpu.make_async_copy(w_o, wo.at[m], w_sem.at[6]),
    ]
    for load in loads:
        load.start()

    cell_row = cells[...].astype(F32)
    diagonal = iota((128, 128), 0) == iota((128, 128), 1)
    lanes = iota((128, 512), 1)
    load_tokens.wait()
    for b in range(4):
        part = cell_row[:, b * 128 : b * 128 + 128]
        col = jnp.sum(jnp.where(diagonal, part, 0.0), axis=1, keepdims=True)
        picked = mm(hot(lanes == col.astype(jnp.int32)), tokens[...])
        x1[b * 32 : b * 32 + 32] = picked.astype(BF16).reshape(32, 4, D)
    pl.semaphore_wait(barrier, ROUNDS - 1 + NX - 1)
    send_rounds(lambda i: x1.at[i], tok, 0)
    tok[me] = x1[me]
    loads[6].wait()
    share_wo = send_x(lambda i: wo.at[m], wo.at[m], 0)

    own_pick = lanes == 4 * me + (iota((128, 512), 0) & 3)
    own_col = jnp.sum(jnp.where(own_pick, cell_row, 0.0), axis=1, keepdims=True)
    obs_all = jnp.concatenate(
        [obs[...].astype(F32), jnp.zeros((112, 512), F32)], axis=0
    ).astype(BF16)
    support = mm_nt(hot(lanes == own_col.astype(jnp.int32)), obs_all)
    divisor = jnp.sqrt(128.0 * mm_nt(jnp.ones((8, 512), BF16), obs_all))[0:1]

    s, o = iota((SLOTS, 128), 0), iota((SLOTS, 128), 1)
    both_rows = jnp.where((s & 1) == 0, seam[0:1], seam[1:2]).astype(F32)
    slot_col = jnp.sum(jnp.where(o == (s >> 1), both_rows, 0.0), axis=1, keepdims=True)
    empty = slot_col < 0.0
    hot_g = hot(iota((SLOTS, ROWS), 1) == slot_col.astype(jnp.int32))
    same = iota((SLOTS, SLOTS), 0) == iota((SLOTS, SLOTS), 1)
    slot_row = jnp.sum(jnp.where(same, slot_col, 0.0), axis=0, keepdims=True)
    hot_t[...] = hot(iota((ROWS, SLOTS), 0) == slot_row.astype(jnp.int32))

    gain_row = gain[...]
    for load in loads[:3]:
        load.wait()
    wait_rounds(tok, r_recv, 0)

    def norm_step(c, carry):
        values = tok[pl.ds(c * 32, 32)].reshape(128, D).astype(F32)
        spread = jnp.mean(values * values, axis=-1, keepdims=True)
        normal = (values * lax.rsqrt(spread + EPS) * gain_row).astype(BF16)
        at = pl.ds(pl.multiple_of(c * 128, 128), 128)
        normed[at, :] = normal
        qkv[at, :] = mm(normal, wqkv[...]).astype(BF16)
        return carry

    lax.fori_loop(0, 4, norm_step, 0)

    sent = mm(hot_g, qkv[...])
    sent = jnp.where((iota((SLOTS, 3 * HD), 1) == 0) & empty, MARK, sent).astype(BF16)
    sx[...] = sent.reshape(ROUNDS, 2, 3 * HD)
    send_rounds(lambda i: sx.at[i], sb, 1)
    sb[me] = sx[me]

    for load in loads[3:6]:
        load.wait()

    def ff_step(i, carry):
        block = normed[pl.ds(pl.multiple_of(i * 128, 128), 128), :]
        gate = mm(block, wg[...])
        up = mm(block, wu[...])
        hidden = (gate * (1.0 / (1.0 + jnp.exp(-gate))) * up).astype(BF16)
        ff[i] = mm(hidden, wd[...])
        return carry

    lax.fori_loop(0, 4, ff_step, 0)
    share_ff = send_x(lambda i: ff.at[i], ffb.at[m], 1)
    ffb[m] = ff[m]

    low = iota((ROWS, HD), 1) < 64
    for h in range(2):
        half = low if h == 0 else jnp.logical_not(low)
        keys = jnp.where(half, qkv[:, HD : 2 * HD], 0.0).astype(BF16)
        values = jnp.where(half, qkv[:, 2 * HD : 3 * HD], 0.0).astype(BF16)
        for blk in range(2):
            at = slice(blk * 256, blk * 256 + 256)
            mix = mm(softmax(mm_nt(qkv[at, 0:HD], keys)), values)
            if h == 0:
                local[at, :] = mix
            else:
                local[at, :] += mix

    wait_rounds(sb, r_recv, 1)
    held = sb[...].reshape(SLOTS, 3 * HD)
    sq = held[:, 0:HD].astype(F32)
    sk, sv = held[:, HD : 2 * HD].astype(F32), held[:, 2 * HD :].astype(F32)
    dead = sq[:, 0:1] > 1e20
    sq = jnp.where(dead, 0.0, sq)
    lane = iota((SLOTS, HD), 1)
    total = jnp.zeros((SLOTS, HD), F32)
    for h in range(2):
        half = lane < 64 if h == 0 else lane >= 64
        spot = lane == (64 if h == 0 else 0)
        queries = jnp.where(half, sq, jnp.where(spot, 1.0, 0.0)).astype(BF16)
        keys = jnp.where(half, sk, jnp.where(spot & dead, DEAD, 0.0)).astype(BF16)
        values = jnp.where(half, sv, 0.0).astype(BF16)
        total += mm(softmax(mm_nt(queries, keys)), values)
    ra[...] = total.astype(BF16).reshape(ROUNDS, 2, HD)
    send_rounds(lambda i: ra.at[i], rb, 2)
    rb[me] = ra[me]

    own_tok = tok[pl.ds(m * 32, 32)].reshape(128, D).astype(F32)
    finish(share_wo)
    finish(share_ff)
    ff_own = ffb[0] + ffb[1] + ffb[2] + ffb[3]
    wait_rounds(rb, r_recv, 2)

    both = local[...] + mm(hot_t[...], rb[...].reshape(SLOTS, HD))
    cx[...] = both.astype(BF16).reshape(NX, 128, HD)
    comb_x = send_x(lambda i: cx.at[i], cb.at[m], 2)
    cb[m] = cx[m]
    finish(comb_x)
    attn = mm(cb[0], wo[0]) + mm(cb[1], wo[1]) + mm(cb[2], wo[2]) + mm(cb[3], wo[3])
    result = (own_tok + (attn + ff_own)).astype(BF16)
    out[...] = result.reshape(32, 4, D)

    dots = jnp.sum(result.astype(F32) * w_r[...], axis=1, keepdims=True)
    px[m] = jnp.sum(support * dots, axis=0, keepdims=True)
    sum_x = send_x(lambda i: px.at[m], px.at[m], 3)
    finish(sum_x)
    pr[me] = jnp.sum(px[...], axis=0)
    send_rounds(lambda i: pr.at[me], pr, 3)
    wait_rounds(pr, r_recv, 3)
    pooled = jnp.sum(pr[...], axis=0)
    logits[...] = (pooled / divisor)[:, 0:16]
    for slot, buffer in enumerate((tok, sb, rb, pr)):
        wait_rounds(buffer, r_send, slot)


def in_hbm(array):
    return pltpu.with_memory_space_constraint(array, pltpu.HBM)


def shards(
    tokens, cell_order, seam_rows, obs_mask, norm_gain,
    w_query, w_key, w_value, w_out, w_gate, w_up, w_down, w_read,
):
    vmem = pl.BlockSpec(memory_space=pltpu.VMEM)
    hbm = pl.BlockSpec(memory_space=pltpu.HBM)
    dma = pltpu.SemaphoreType.DMA
    V = pltpu.VMEM
    out, logits = pl.pallas_call(
        kernel,
        out_shape=(
            jax.ShapeDtypeStruct((32, 4, D), BF16),
            jax.ShapeDtypeStruct((1, 16), F32),
        ),
        in_specs=[hbm] + [vmem] * 4 + [hbm] * 7 + [vmem],
        out_specs=(vmem, vmem),
        scratch_shapes=[
            V((D, D), BF16), V((D, 3 * HD), BF16), V((NX, HD, D), BF16),
            V((D, D), BF16), V((D, D), BF16), V((D, D), BF16),
            V((ROUNDS, 4, D), BF16), V((ROUNDS, 4, D), BF16), V((ROWS, D), BF16),
            V((ROWS, 3 * HD), BF16), V((ROWS, HD), F32),
            V((ROUNDS, 2, 3 * HD), BF16), V((ROUNDS, 2, 3 * HD), BF16),
            V((ROUNDS, 2, HD), BF16), V((ROUNDS, 2, HD), BF16),
            V((ROWS, SLOTS), BF16), V((NX, 128, D), F32), V((NX, 128, D), F32),
            V((NX, 128, HD), BF16), V((NX, 128, HD), BF16),
            V((NX, 1, 128), F32), V((ROUNDS, 1, 128), F32),
            dma((8,)), dma((4,)), dma((4,)), dma((4, NX)), dma((4, NX)),
        ],
        compiler_params=pltpu.CompilerParams(
            collective_id=0, has_side_effects=True, vmem_limit_bytes=40 * 2 ** 20
        ),
    )(
        in_hbm(tokens.reshape(512, D)), cell_order.reshape(1, 512), seam_rows[0].T,
        obs_mask, norm_gain.reshape(1, D),
        *[in_hbm(w) for w in (w_query, w_key, w_value, w_out, w_gate, w_up, w_down)],
        w_read.reshape(1, D),
    )
    return out, logits.reshape(16)


def solution(mesh):
    return jax.shard_map(
        shards,
        mesh=mesh,
        in_specs=(
            P("round", None, None),
            P(),
            P("round", None, None),
            P(),
            P(),
            P(None, "mp"),
            P(None, "mp"),
            P(None, "mp"),
            P("mp", None),
            P(None, "mp"),
            P(None, "mp"),
            P("mp", None),
            P(),
        ),
        out_specs=(P("mp", "round", None), P()),
        check_vma=False,
    )
```

```python
import jax
import jax.numpy as jnp
from jax import lax
from jax.experimental import pallas as pl
from jax.experimental.pallas import tpu as pltpu
from jax.sharding import PartitionSpec as P

F32 = jnp.float32
BF16 = jnp.bfloat16
MESH = pl.DeviceIdType.MESH
EPS = 1e-6
TURNS = (7, 6, 5, 4, 3, 2, 1, 0)
ROUNDS, NX = 128, 4
ORDER = (4, 3, 5, 2, 6, 1, 7, 0)


def distance(k):
    return 4 + (1 - 2 * lax.rem(k, 2)) * ((k + 1) // 2)

D, HD, ROWS, SLOTS = 512, 128, 512, 256
MARK = 2.0 ** 100
DEAD = -1e30


def iota(shape, axis):
    return lax.broadcasted_iota(jnp.int32, shape, axis)


def hot(mask):
    return jnp.where(mask, 1.0, 0.0).astype(BF16)


def mm(a, b):
    return jnp.dot(a, b, preferred_element_type=F32)


def mm_nt(a, b):
    return lax.dot_general(a, b, (((1,), (1,)), ((), ())), preferred_element_type=F32)


def softmax(scores):
    top = jnp.max(scores, axis=-1, keepdims=True)
    weights = jnp.exp((scores - top) * 0.125)
    total = jnp.sum(weights, axis=-1, keepdims=True)
    return (weights * (1.0 / total)).astype(BF16)


def kernel(
    tokens_hbm, cells_hbm, seam_hbm, obs_hbm, gain_hbm,
    w_q, w_k, w_v, w_o, w_g, w_u, w_d, w_r_hbm,
    out, logits,
    tokens, cells, seam, obs, gain, w_r, wqkv, wo, wg, wu, wd,
    x1, tok, normed, qkv, local, sx, sb, ra, rb, hot_t, ff, ffb, cx, cb, px, pr,
    w_sem, r_send, r_recv, x_send, x_recv, t_send, t_recv, tx_send, tx_recv,
):
    me = lax.axis_index("round")
    m = lax.axis_index("mp")
    z, y, core = me // 16, lax.rem(me // 2, 8), lax.rem(me, 2)

    def z_of(k):
        return lax.rem(z + distance(k), 8) * 16

    columns = [
        lax.rem(y + d, 8) * 2 + (c if swap else 1 - c)
        for d in ORDER
        for swap, c in ((False, core), (True, core))
    ]

    def each_round(act):
        def turn(k, carry):
            plane = z_of(k)
            for column in columns:
                act(plane + column, k)
            return carry

        lax.fori_loop(0, 7, turn, 0)
        for column in columns[:15]:
            act(z * 16 + column, 7)

    def x_peer(k):
        return lax.rem(m + k, NX)

    def send_rounds(src, dst, slot):
        def act(to, turn):
            pltpu.make_async_remote_copy(
                src_ref=src(to),
                dst_ref=dst.at[me],
                send_sem=r_send.at[slot],
                recv_sem=r_recv.at[slot],
                device_id=(to, m),
                device_id_type=MESH,
            ).start()

        each_round(act)

    def wait_rounds(buffer, sem, slot):
        others = buffer.at[pl.ds(0, ROUNDS - 1)]
        pltpu.make_async_copy(others, others, sem.at[slot]).wait()

    def send_x(src, dst, slot):
        started = []
        for k in (2, 1, 3):
            to = x_peer(k)
            copy = pltpu.make_async_remote_copy(
                src_ref=src(to),
                dst_ref=dst,
                send_sem=x_send.at[slot, k],
                recv_sem=x_recv.at[slot, k],
                device_id=(me, to),
                device_id_type=MESH,
            )
            copy.start()
            started.append(copy)
        return started

    def finish(started):
        for copy in started:
            copy.wait()

    chunk = pl.ds(pl.multiple_of(m * 128, 128), 128)
    first = [
        pltpu.make_async_copy(cells_hbm, cells, w_sem.at[7]),
        pltpu.make_async_copy(tokens_hbm.at[:, chunk], tokens, w_sem.at[8]),
        pltpu.make_async_copy(seam_hbm, seam, w_sem.at[9]),
        pltpu.make_async_copy(obs_hbm, obs, w_sem.at[10]),
        pltpu.make_async_copy(gain_hbm, gain, w_sem.at[11]),
        pltpu.make_async_copy(w_r_hbm, w_r, w_sem.at[12]),
    ]
    for load in first:
        load.start()
    barrier = pltpu.get_barrier_semaphore()

    def greet(to, turn):
        pl.semaphore_signal(barrier, inc=1, device_id=(to, m), device_id_type=MESH)

    each_round(greet)
    for k in range(1, NX):
        pl.semaphore_signal(
            barrier, inc=1, device_id=(me, x_peer(k)), device_id_type=MESH
        )

    loads = [
        pltpu.make_async_copy(w_q, wqkv.at[:, pl.ds(0, HD)], w_sem.at[0]),
        pltpu.make_async_copy(w_k, wqkv.at[:, pl.ds(HD, HD)], w_sem.at[1]),
        pltpu.make_async_copy(w_v, wqkv.at[:, pl.ds(2 * HD, HD)], w_sem.at[2]),
        pltpu.make_async_copy(w_g, wg, w_sem.at[3]),
        pltpu.make_async_copy(w_u, wu, w_sem.at[4]),
        pltpu.make_async_copy(w_d, wd, w_sem.at[5]),
        pltpu.make_async_copy(w_o, wo.at[m], w_sem.at[6]),
    ]
    for load in loads:
        load.start()

    for load in first:
        load.wait()
    cell_row = cells[...].astype(F32)
    diagonal = iota((128, 128), 0) == iota((128, 128), 1)
    lanes = iota((128, 512), 1)
    for b in range(4):
        part = cell_row[:, b * 128 : b * 128 + 128]
        col = jnp.sum(jnp.where(diagonal, part, 0.0), axis=1, keepdims=True)
        picked = mm(hot(lanes == col.astype(jnp.int32)), tokens[...])
        x1[b * 32 : b * 32 + 32] = picked.astype(BF16).reshape(32, 4, 128)
    pl.semaphore_wait(barrier, ROUNDS - 1 + NX - 1)

    def send_tokens(to, turn):
        pltpu.make_async_remote_copy(
            src_ref=x1.at[to],
            dst_ref=tok.at[m, me],
            send_sem=t_send,
            recv_sem=t_recv.at[turn],
            device_id=(to, m),
            device_id_type=MESH,
        ).start()

    each_round(send_tokens)
    tok[m, me] = x1[me]
    loads[6].wait()
    share_wo = send_x(lambda i: wo.at[m], wo.at[m], 0)

    own_pick = lanes == 4 * me + (iota((128, 512), 0) & 3)
    own_col = jnp.sum(jnp.where(own_pick, cell_row, 0.0), axis=1, keepdims=True)
    obs_all = jnp.concatenate(
        [obs[...].astype(F32), jnp.zeros((112, 512), F32)], axis=0
    ).astype(BF16)
    support = mm_nt(hot(lanes == own_col.astype(jnp.int32)), obs_all)
    divisor = jnp.sqrt(128.0 * mm_nt(jnp.ones((8, 512), BF16), obs_all))[0:1]

    s, o = iota((SLOTS, 128), 0), iota((SLOTS, 128), 1)
    both_rows = jnp.where((s & 1) == 0, seam[0:1], seam[1:2]).astype(F32)
    slot_col = jnp.sum(jnp.where(o == (s >> 1), both_rows, 0.0), axis=1, keepdims=True)
    empty = slot_col < 0.0
    hot_g = hot(iota((SLOTS, ROWS), 1) == slot_col.astype(jnp.int32))
    same = iota((SLOTS, SLOTS), 0) == iota((SLOTS, SLOTS), 1)
    slot_row = jnp.sum(jnp.where(same, slot_col, 0.0), axis=0, keepdims=True)
    hot_t[...] = hot(iota((ROWS, SLOTS), 0) == slot_row.astype(jnp.int32))

    gain_row = gain[...]
    for load in loads[:3]:
        load.wait()
    forwards = []
    for k in TURNS:
        from_z = lax.rem(z + 8 - ORDER[k], 8) * 16
        plane = tok.at[m, pl.ds(from_z, 16)]
        landed = plane if k < 7 else tok.at[m, pl.ds(0, 15)]
        pltpu.make_async_copy(landed, landed, t_recv.at[k]).wait()
        for i in (2, 1, 3):
            copy = pltpu.make_async_remote_copy(
                src_ref=plane,
                dst_ref=plane,
                send_sem=tx_send.at[k, i],
                recv_sem=tx_recv.at[k, i],
                device_id=(me, x_peer(i)),
                device_id_type=MESH,
            )
            copy.start()
            forwards.append(copy)
    for copy in forwards:
        copy.wait_recv()

    def norm_step(c, carry):
        at = pl.ds(c * 32, 32)
        values = jnp.concatenate(
            [tok[i, at].reshape(128, 128) for i in range(NX)], axis=1
        ).astype(F32)
        spread = jnp.mean(values * values, axis=-1, keepdims=True)
        normal = (values * lax.rsqrt(spread + EPS) * gain_row).astype(BF16)
        at = pl.ds(pl.multiple_of(c * 128, 128), 128)
        normed[at, :] = normal
        qkv[at, :] = mm(normal, wqkv[...]).astype(BF16)
        return carry

    lax.fori_loop(0, 4, norm_step, 0)

    sent = mm(hot_g, qkv[...])
    sent = jnp.where((iota((SLOTS, 3 * HD), 1) == 0) & empty, MARK, sent).astype(BF16)
    sx[...] = sent.reshape(ROUNDS, 2, 3 * HD)
    send_rounds(lambda i: sx.at[i], sb, 1)
    sb[me] = sx[me]

    for load in loads[3:6]:
        load.wait()

    def ff_step(i, carry):
        block = normed[pl.ds(pl.multiple_of(i * 128, 128), 128), :]
        gate = mm(block, wg[...])
        up = mm(block, wu[...])
        hidden = (gate * (1.0 / (1.0 + jnp.exp(-gate))) * up).astype(BF16)
        ff[i] = mm(hidden, wd[...])
        return carry

    lax.fori_loop(0, 4, ff_step, 0)
    share_ff = send_x(lambda i: ff.at[i], ffb.at[m], 1)
    ffb[m] = ff[m]

    low = iota((ROWS, HD), 1) < 64
    for h in range(2):
        half = low if h == 0 else jnp.logical_not(low)
        keys = jnp.where(half, qkv[:, HD : 2 * HD], 0.0).astype(BF16)
        values = jnp.where(half, qkv[:, 2 * HD : 3 * HD], 0.0).astype(BF16)
        for blk in range(2):
            at = slice(blk * 256, blk * 256 + 256)
            mix = mm(softmax(mm_nt(qkv[at, 0:HD], keys)), values)
            if h == 0:
                local[at, :] = mix
            else:
                local[at, :] += mix

    wait_rounds(sb, r_recv, 1)
    held = sb[...].reshape(SLOTS, 3 * HD)
    sq = held[:, 0:HD].astype(F32)
    sk, sv = held[:, HD : 2 * HD].astype(F32), held[:, 2 * HD :].astype(F32)
    dead = sq[:, 0:1] > 1e20
    sq = jnp.where(dead, 0.0, sq)
    lane = iota((SLOTS, HD), 1)
    total = jnp.zeros((SLOTS, HD), F32)
    for h in range(2):
        half = lane < 64 if h == 0 else lane >= 64
        spot = lane == (64 if h == 0 else 0)
        queries = jnp.where(half, sq, jnp.where(spot, 1.0, 0.0)).astype(BF16)
        keys = jnp.where(half, sk, jnp.where(spot & dead, DEAD, 0.0)).astype(BF16)
        values = jnp.where(half, sv, 0.0).astype(BF16)
        total += mm(softmax(mm_nt(queries, keys)), values)
    ra[...] = total.astype(BF16).reshape(ROUNDS, 2, HD)
    send_rounds(lambda i: ra.at[i], rb, 2)
    rb[me] = ra[me]

    own_tok = jnp.concatenate(
        [tok[i, pl.ds(m * 32, 32)].reshape(128, 128) for i in range(NX)], axis=1
    ).astype(F32)
    finish(share_wo)
    finish(share_ff)
    ff_own = ffb[0] + ffb[1] + ffb[2] + ffb[3]
    wait_rounds(rb, r_recv, 2)

    both = local[...] + mm(hot_t[...], rb[...].reshape(SLOTS, HD))
    cx[...] = both.astype(BF16).reshape(NX, 128, HD)
    comb_x = send_x(lambda i: cx.at[i], cb.at[m], 2)
    cb[m] = cx[m]
    finish(comb_x)
    attn = mm(cb[0], wo[0]) + mm(cb[1], wo[1]) + mm(cb[2], wo[2]) + mm(cb[3], wo[3])
    result = (own_tok + (attn + ff_own)).astype(BF16)
    out[...] = result.reshape(32, 4, D)

    dots = jnp.sum(result.astype(F32) * w_r[...], axis=1, keepdims=True)
    px[m] = jnp.sum(support * dots, axis=0, keepdims=True)
    sum_x = send_x(lambda i: px.at[m], px.at[m], 3)
    finish(sum_x)
    pr[me] = jnp.sum(px[...], axis=0)
    send_rounds(lambda i: pr.at[me], pr, 3)
    wait_rounds(pr, r_recv, 3)
    pooled = jnp.sum(pr[...], axis=0)
    logits[...] = (pooled / divisor)[:, 0:16]
    for slot, buffer in ((1, sb), (2, rb), (3, pr)):
        wait_rounds(buffer, r_send, slot)
    sent_tokens = x1.at[pl.ds(0, ROUNDS - 1)]
    pltpu.make_async_copy(sent_tokens, sent_tokens, t_send).wait()
    for copy in forwards:
        copy.wait_send()


def in_hbm(array):
    return pltpu.with_memory_space_constraint(array, pltpu.HBM)


def shards(
    tokens, cell_order, seam_rows, obs_mask, norm_gain,
    w_query, w_key, w_value, w_out, w_gate, w_up, w_down, w_read,
):
    vmem = pl.BlockSpec(memory_space=pltpu.VMEM)
    hbm = pl.BlockSpec(memory_space=pltpu.HBM)
    dma = pltpu.SemaphoreType.DMA
    V = pltpu.VMEM
    out, logits = pl.pallas_call(
        kernel,
        out_shape=(
            jax.ShapeDtypeStruct((32, 4, D), BF16),
            jax.ShapeDtypeStruct((1, 16), F32),
        ),
        in_specs=[hbm] * 13,
        out_specs=(vmem, vmem),
        scratch_shapes=[
            V((D, 128), BF16), V((1, 512), jnp.int32), V((2, 128), jnp.int32),
            V((16, 512), jnp.int32), V((1, D), F32), V((1, D), F32),
            V((D, 3 * HD), BF16), V((NX, HD, D), BF16),
            V((D, D), BF16), V((D, D), BF16), V((D, D), BF16),
            V((ROUNDS, 4, 128), BF16), V((NX, ROUNDS, 4, 128), BF16), V((ROWS, D), BF16),
            V((ROWS, 3 * HD), BF16), V((ROWS, HD), F32),
            V((ROUNDS, 2, 3 * HD), BF16), V((ROUNDS, 2, 3 * HD), BF16),
            V((ROUNDS, 2, HD), BF16), V((ROUNDS, 2, HD), BF16),
            V((ROWS, SLOTS), BF16), V((NX, 128, D), F32), V((NX, 128, D), F32),
            V((NX, 128, HD), BF16), V((NX, 128, HD), BF16),
            V((NX, 1, 128), F32), V((ROUNDS, 1, 128), F32),
            dma((13,)), dma((4,)), dma((4,)), dma((4, NX)), dma((4, NX)),
            dma, dma((8,)), dma((8, NX)), dma((8, NX)),
        ],
        compiler_params=pltpu.CompilerParams(
            collective_id=0, has_side_effects=True, vmem_limit_bytes=40 * 2 ** 20
        ),
    )(
        *[
            in_hbm(array)
            for array in (
                tokens.reshape(512, D), cell_order.reshape(1, 512), seam_rows[0].T,
                obs_mask, norm_gain.reshape(1, D), w_query, w_key, w_value, w_out,
                w_gate, w_up, w_down, w_read.reshape(1, D),
            )
        ]
    )
    return out, logits.reshape(16)


def solution(mesh):
    return jax.shard_map(
        shards,
        mesh=mesh,
        in_specs=(
            P("round", None, None),
            P(),
            P("round", None, None),
            P(),
            P(),
            P(None, "mp"),
            P(None, "mp"),
            P(None, "mp"),
            P("mp", None),
            P(None, "mp"),
            P(None, "mp"),
            P("mp", None),
            P(),
        ),
        out_specs=(P("mp", "round", None), P()),
        check_vma=False,
    )
```

```python
import jax
import jax.numpy as jnp
from jax import lax
from jax.experimental import pallas as pl
from jax.experimental.pallas import tpu as pltpu
from jax.sharding import PartitionSpec as P

F32 = jnp.float32
BF16 = jnp.bfloat16
MESH = pl.DeviceIdType.MESH
EPS = 1e-6
TURNS = (7, 6, 5, 4, 3, 2, 1, 0)
ROUNDS, NX = 128, 4
ORDER = (4, 3, 5, 2, 6, 1, 7, 0)


def distance(k):
    return 4 + (1 - 2 * lax.rem(k, 2)) * ((k + 1) // 2)

D, HD, ROWS, SLOTS = 512, 128, 512, 256
MARK = 2.0 ** 100
DEAD = -1e30


def iota(shape, axis):
    return lax.broadcasted_iota(jnp.int32, shape, axis)


def hot(mask):
    return jnp.where(mask, 1.0, 0.0).astype(BF16)


def mm(a, b):
    return jnp.dot(a, b, preferred_element_type=F32)


def mm_nt(a, b):
    return lax.dot_general(a, b, (((1,), (1,)), ((), ())), preferred_element_type=F32)


def softmax(scores):
    top = jnp.max(scores, axis=-1, keepdims=True)
    weights = jnp.exp((scores - top) * 0.125)
    total = jnp.sum(weights, axis=-1, keepdims=True)
    return (weights * (1.0 / total)).astype(BF16)


def kernel(
    tokens_hbm, cells_hbm, seam_hbm, obs_hbm, gain_hbm,
    w_q, w_k, w_v, w_o, w_g, w_u, w_d, w_r_hbm,
    out, logits,
    tokens, cells, seam, obs, gain, w_r, wqkv, wo, wg, wu, wd,
    x1, tok, normed, qkv, local, sx, sb, ra, rb, hot_t, ff, ffb, cx, cb, px, pr,
    w_sem, r_send, r_recv, x_send, x_recv, p_send, p_recv, t_send, t_recv, tx_send, tx_recv,
):
    me = lax.axis_index("round")
    m = lax.axis_index("mp")
    z, y, core = me // 16, lax.rem(me // 2, 8), lax.rem(me, 2)

    def z_of(k):
        return lax.rem(z + distance(k), 8) * 16

    columns = [
        lax.rem(y + d, 8) * 2 + (c if swap else 1 - c)
        for d in ORDER
        for swap, c in ((False, core), (True, core))
    ]

    def each_round(act):
        def turn(k, carry):
            plane = z_of(k)
            for column in columns:
                act(plane + column, k)
            return carry

        lax.fori_loop(0, 7, turn, 0)
        for column in columns[:15]:
            act(z * 16 + column, 7)

    def x_peer(k):
        return lax.rem(m + k, NX)

    def near_peer(k):
        return me + (1 - 2 * core) * (k % 2), x_peer(k // 2)

    def send_rounds(src, dst, slot):
        def act(to, turn):
            pltpu.make_async_remote_copy(
                src_ref=src(to),
                dst_ref=dst.at[me],
                send_sem=r_send.at[slot],
                recv_sem=r_recv.at[slot],
                device_id=(to, m),
                device_id_type=MESH,
            ).start()

        each_round(act)

    def wait_rounds(buffer, sem, slot):
        others = buffer.at[pl.ds(0, ROUNDS - 1)]
        pltpu.make_async_copy(others, others, sem.at[slot]).wait()

    def send_x(src, dst, slot):
        started = []
        for k in (2, 1, 3):
            to = x_peer(k)
            copy = pltpu.make_async_remote_copy(
                src_ref=src(to),
                dst_ref=dst,
                send_sem=x_send.at[slot, k],
                recv_sem=x_recv.at[slot, k],
                device_id=(me, to),
                device_id_type=MESH,
            )
            copy.start()
            started.append(copy)
        return started

    def finish(started):
        for copy in started:
            copy.wait()

    chunk = pl.ds(pl.multiple_of(m * 128, 128), 128)
    first = [
        pltpu.make_async_copy(cells_hbm, cells, w_sem.at[7]),
        pltpu.make_async_copy(tokens_hbm.at[:, chunk], tokens, w_sem.at[8]),
        pltpu.make_async_copy(seam_hbm, seam, w_sem.at[9]),
        pltpu.make_async_copy(obs_hbm, obs, w_sem.at[10]),
        pltpu.make_async_copy(gain_hbm, gain, w_sem.at[11]),
        pltpu.make_async_copy(w_r_hbm, w_r, w_sem.at[12]),
    ]
    barrier = pltpu.get_barrier_semaphore()

    def greet(to, turn):
        pl.semaphore_signal(barrier, inc=1, device_id=(to, m), device_id_type=MESH)

    each_round(greet)
    for k in range(2, 8):
        pl.semaphore_signal(
            barrier, inc=1, device_id=near_peer(k), device_id_type=MESH
        )

    for load in first:
        load.start()

    loads = [
        pltpu.make_async_copy(w_q, wqkv.at[:, pl.ds(0, HD)], w_sem.at[0]),
        pltpu.make_async_copy(w_k, wqkv.at[:, pl.ds(HD, HD)], w_sem.at[1]),
        pltpu.make_async_copy(w_v, wqkv.at[:, pl.ds(2 * HD, HD)], w_sem.at[2]),
        pltpu.make_async_copy(w_g, wg, w_sem.at[3]),
        pltpu.make_async_copy(w_u, wu, w_sem.at[4]),
        pltpu.make_async_copy(w_d, wd, w_sem.at[5]),
        pltpu.make_async_copy(w_o, wo.at[m], w_sem.at[6]),
    ]
    for load in loads:
        load.start()

    for load in first:
        load.wait()
    cell_row = cells[...].astype(F32)
    diagonal = iota((128, 128), 0) == iota((128, 128), 1)
    lanes = iota((128, 512), 1)
    for b in range(4):
        part = cell_row[:, b * 128 : b * 128 + 128]
        col = jnp.sum(jnp.where(diagonal, part, 0.0), axis=1, keepdims=True)
        picked = mm(hot(lanes == col.astype(jnp.int32)), tokens[...])
        x1[b * 32 : b * 32 + 32] = picked.astype(BF16).reshape(32, 4, 128)
    pl.semaphore_wait(barrier, ROUNDS - 1 + 6)

    def send_tokens(to, turn):
        pltpu.make_async_remote_copy(
            src_ref=x1.at[to],
            dst_ref=tok.at[m, me],
            send_sem=t_send,
            recv_sem=t_recv.at[turn],
            device_id=(to, m),
            device_id_type=MESH,
        ).start()

    each_round(send_tokens)
    tok[m, me] = x1[me]
    loads[6].wait()
    share_wo = send_x(lambda i: wo.at[m], wo.at[m], 0)

    own_pick = lanes == 4 * me + (iota((128, 512), 0) & 3)
    own_col = jnp.sum(jnp.where(own_pick, cell_row, 0.0), axis=1, keepdims=True)
    obs_all = jnp.concatenate(
        [obs[...].astype(F32), jnp.zeros((112, 512), F32)], axis=0
    ).astype(BF16)
    support = mm_nt(hot(lanes == own_col.astype(jnp.int32)), obs_all)
    divisor = jnp.sqrt(128.0 * mm_nt(jnp.ones((8, 512), BF16), obs_all))[0:1]

    s, o = iota((SLOTS, 128), 0), iota((SLOTS, 128), 1)
    both_rows = jnp.where((s & 1) == 0, seam[0:1], seam[1:2]).astype(F32)
    slot_col = jnp.sum(jnp.where(o == (s >> 1), both_rows, 0.0), axis=1, keepdims=True)
    empty = slot_col < 0.0
    hot_g = hot(iota((SLOTS, ROWS), 1) == slot_col.astype(jnp.int32))
    same = iota((SLOTS, SLOTS), 0) == iota((SLOTS, SLOTS), 1)
    slot_row = jnp.sum(jnp.where(same, slot_col, 0.0), axis=0, keepdims=True)
    hot_t[...] = hot(iota((ROWS, SLOTS), 0) == slot_row.astype(jnp.int32))

    gain_row = gain[...]
    for load in loads[:3]:
        load.wait()
    forwards = []
    for k in TURNS:
        from_z = lax.rem(z + 8 - ORDER[k], 8) * 16
        plane = tok.at[m, pl.ds(from_z, 16)]
        landed = plane if k < 7 else tok.at[m, pl.ds(0, 15)]
        pltpu.make_async_copy(landed, landed, t_recv.at[k]).wait()
        for i in (2, 1, 3):
            copy = pltpu.make_async_remote_copy(
                src_ref=plane,
                dst_ref=plane,
                send_sem=tx_send.at[k, i],
                recv_sem=tx_recv.at[k, i],
                device_id=(me, x_peer(i)),
                device_id_type=MESH,
            )
            copy.start()
            forwards.append(copy)
    for n, k in enumerate(TURNS):
        for copy in forwards[3 * n : 3 * n + 3]:
            copy.wait_recv()
        from_z = lax.rem(z + 8 - ORDER[k], 8)
        at = pl.ds(from_z * 16, 16)
        values = jnp.concatenate(
            [tok[i, at].reshape(64, 128) for i in range(NX)], axis=1
        ).astype(F32)
        spread = jnp.mean(values * values, axis=-1, keepdims=True)
        normal = (values * lax.rsqrt(spread + EPS) * gain_row).astype(BF16)
        normed[pl.ds(pl.multiple_of(from_z * 64, 64), 64), :] = normal
    qkv[...] = mm(normed[...], wqkv[...]).astype(BF16)

    sent = mm(hot_g, qkv[...])
    sent = jnp.where((iota((SLOTS, 3 * HD), 1) == 0) & empty, MARK, sent).astype(BF16)
    sx[...] = sent.reshape(ROUNDS, 2, 3 * HD)
    send_rounds(lambda i: sx.at[i], sb, 1)
    sb[me] = sx[me]

    for load in loads[3:6]:
        load.wait()

    def ff_step(i, carry):
        block = normed[pl.ds(pl.multiple_of(i * 128, 128), 128), :]
        gate = mm(block, wg[...])
        up = mm(block, wu[...])
        hidden = (gate * (1.0 / (1.0 + jnp.exp(-gate))) * up).astype(BF16)
        ff[i] = mm(hidden, wd[...])
        return carry

    lax.fori_loop(0, 4, ff_step, 0)
    share_ff = send_x(lambda i: ff.at[i], ffb.at[m], 1)
    ffb[m] = ff[m]

    low = iota((ROWS, HD), 1) < 64
    for h in range(2):
        half = low if h == 0 else jnp.logical_not(low)
        keys = jnp.where(half, qkv[:, HD : 2 * HD], 0.0).astype(BF16)
        values = jnp.where(half, qkv[:, 2 * HD : 3 * HD], 0.0).astype(BF16)
        for blk in range(2):
            at = slice(blk * 256, blk * 256 + 256)
            mix = mm(softmax(mm_nt(qkv[at, 0:HD], keys)), values)
            if h == 0:
                local[at, :] = mix
            else:
                local[at, :] += mix

    wait_rounds(sb, r_recv, 1)
    held = sb[...].reshape(SLOTS, 3 * HD)
    sq = held[:, 0:HD].astype(F32)
    sk, sv = held[:, HD : 2 * HD].astype(F32), held[:, 2 * HD :].astype(F32)
    dead = sq[:, 0:1] > 1e20
    sq = jnp.where(dead, 0.0, sq)
    lane = iota((SLOTS, HD), 1)
    total = jnp.zeros((SLOTS, HD), F32)
    for h in range(2):
        half = lane < 64 if h == 0 else lane >= 64
        spot = lane == (64 if h == 0 else 0)
        queries = jnp.where(half, sq, jnp.where(spot, 1.0, 0.0)).astype(BF16)
        keys = jnp.where(half, sk, jnp.where(spot & dead, DEAD, 0.0)).astype(BF16)
        values = jnp.where(half, sv, 0.0).astype(BF16)
        total += mm(softmax(mm_nt(queries, keys)), values)
    ra[...] = total.astype(BF16).reshape(ROUNDS, 2, HD)
    send_rounds(lambda i: ra.at[i], rb, 2)
    rb[me] = ra[me]

    own_tok = jnp.concatenate(
        [tok[i, pl.ds(m * 32, 32)].reshape(128, 128) for i in range(NX)], axis=1
    ).astype(F32)
    finish(share_wo)
    finish(share_ff)
    ff_own = ffb[0] + ffb[1] + ffb[2] + ffb[3]
    wait_rounds(rb, r_recv, 2)

    both = local[...] + mm(hot_t[...], rb[...].reshape(SLOTS, HD))
    cx[...] = both.astype(BF16).reshape(NX, 128, HD)
    comb_x = send_x(lambda i: cx.at[i], cb.at[m], 2)
    cb[m] = cx[m]
    finish(comb_x)
    attn = mm(cb[0], wo[0]) + mm(cb[1], wo[1]) + mm(cb[2], wo[2]) + mm(cb[3], wo[3])
    result = (own_tok + (attn + ff_own)).astype(BF16)
    out[...] = result.reshape(32, 4, D)

    dots = jnp.sum(result.astype(F32) * w_r[...], axis=1, keepdims=True)
    px[2 * m + core] = jnp.sum(support * dots, axis=0, keepdims=True)
    sums = []
    for k in range(1, 8):
        copy = pltpu.make_async_remote_copy(
            src_ref=px.at[2 * m + core],
            dst_ref=px.at[2 * m + core],
            send_sem=p_send.at[k],
            recv_sem=p_recv.at[k],
            device_id=near_peer(k),
            device_id_type=MESH,
        )
        copy.start()
        sums.append(copy)
    finish(sums)
    chip = z * 8 + y
    pr[chip] = jnp.sum(px[...], axis=0)

    def send_sum(plane, column):
        pltpu.make_async_remote_copy(
            src_ref=pr.at[chip],
            dst_ref=pr.at[chip],
            send_sem=r_send.at[3],
            recv_sem=r_recv.at[3],
            device_id=(plane + column, m),
            device_id_type=MESH,
        ).start()

    same_core = columns[1::2]

    def sum_turn(k, carry):
        plane = z_of(k)
        for column in same_core:
            send_sum(plane, column)
        return carry

    lax.fori_loop(0, 7, sum_turn, 0)
    for column in same_core[:7]:
        send_sum(z * 16, column)
    others = pr.at[pl.ds(0, 63)]
    pltpu.make_async_copy(others, others, r_recv.at[3]).wait()
    pooled = jnp.sum(pr[...], axis=0)
    logits[...] = (pooled / divisor)[:, 0:16]
    for slot, buffer in ((1, sb), (2, rb)):
        wait_rounds(buffer, r_send, slot)
    sent_tokens = x1.at[pl.ds(0, ROUNDS - 1)]
    pltpu.make_async_copy(sent_tokens, sent_tokens, t_send).wait()
    pltpu.make_async_copy(others, others, r_send.at[3]).wait()
    for copy in forwards:
        copy.wait_send()


def in_hbm(array):
    return pltpu.with_memory_space_constraint(array, pltpu.HBM)


def shards(
    tokens, cell_order, seam_rows, obs_mask, norm_gain,
    w_query, w_key, w_value, w_out, w_gate, w_up, w_down, w_read,
):
    vmem = pl.BlockSpec(memory_space=pltpu.VMEM)
    hbm = pl.BlockSpec(memory_space=pltpu.HBM)
    dma = pltpu.SemaphoreType.DMA
    V = pltpu.VMEM
    out, logits = pl.pallas_call(
        kernel,
        out_shape=(
            jax.ShapeDtypeStruct((32, 4, D), BF16),
            jax.ShapeDtypeStruct((1, 16), F32),
        ),
        in_specs=[hbm] * 13,
        out_specs=(vmem, vmem),
        scratch_shapes=[
            V((D, 128), BF16), V((1, 512), jnp.int32), V((2, 128), jnp.int32),
            V((16, 512), jnp.int32), V((1, D), F32), V((1, D), F32),
            V((D, 3 * HD), BF16), V((NX, HD, D), BF16),
            V((D, D), BF16), V((D, D), BF16), V((D, D), BF16),
            V((ROUNDS, 4, 128), BF16), V((NX, ROUNDS, 4, 128), BF16), V((ROWS, D), BF16),
            V((ROWS, 3 * HD), BF16), V((ROWS, HD), F32),
            V((ROUNDS, 2, 3 * HD), BF16), V((ROUNDS, 2, 3 * HD), BF16),
            V((ROUNDS, 2, HD), BF16), V((ROUNDS, 2, HD), BF16),
            V((ROWS, SLOTS), BF16), V((NX, 128, D), F32), V((NX, 128, D), F32),
            V((NX, 128, HD), BF16), V((NX, 128, HD), BF16),
            V((8, 1, 128), F32), V((64, 1, 128), F32),
            dma((13,)), dma((4,)), dma((4,)), dma((3, NX)), dma((3, NX)),
            dma((8,)), dma((8,)),
            dma, dma((8,)), dma((8, NX)), dma((8, NX)),
        ],
        compiler_params=pltpu.CompilerParams(
            collective_id=0, has_side_effects=True, vmem_limit_bytes=40 * 2 ** 20
        ),
    )(
        *[
            in_hbm(array)
            for array in (
                tokens.reshape(512, D), cell_order.reshape(1, 512), seam_rows[0].T,
                obs_mask, norm_gain.reshape(1, D), w_query, w_key, w_value, w_out,
                w_gate, w_up, w_down, w_read.reshape(1, D),
            )
        ]
    )
    return out, logits.reshape(16)


def solution(mesh):
    return jax.shard_map(
        shards,
        mesh=mesh,
        in_specs=(
            P("round", None, None),
            P(),
            P("round", None, None),
            P(),
            P(),
            P(None, "mp"),
            P(None, "mp"),
            P(None, "mp"),
            P("mp", None),
            P(None, "mp"),
            P(None, "mp"),
            P("mp", None),
            P(),
        ),
        out_specs=(P("mp", "round", None), P()),
        check_vma=False,
    )
```

```python
import jax
import jax.numpy as jnp
from jax import lax
from jax.experimental import pallas as pl
from jax.experimental.pallas import tpu as pltpu
from jax.sharding import PartitionSpec as P

F32 = jnp.float32
BF16 = jnp.bfloat16
MESH = pl.DeviceIdType.MESH
EPS = 1e-6
TURNS = (7, 6, 5, 4, 3, 2, 1, 0)
ROUNDS, NX = 128, 4
ORDER = (4, 3, 5, 2, 6, 1, 7, 0)


def distance(k):
    return 4 + (1 - 2 * lax.rem(k, 2)) * ((k + 1) // 2)

D, HD, ROWS, SLOTS = 512, 128, 512, 256
MARK = 2.0 ** 100
DEAD = -1e30


def iota(shape, axis):
    return lax.broadcasted_iota(jnp.int32, shape, axis)


def hot(mask):
    return jnp.where(mask, 1.0, 0.0).astype(BF16)


def mm(a, b):
    return jnp.dot(a, b, preferred_element_type=F32)


def mm_nt(a, b):
    return lax.dot_general(a, b, (((1,), (1,)), ((), ())), preferred_element_type=F32)


def softmax(scores):
    top = jnp.max(scores, axis=-1, keepdims=True)
    weights = jnp.exp((scores - top) * 0.125)
    total = jnp.sum(weights, axis=-1, keepdims=True)
    return (weights * (1.0 / total)).astype(BF16)


def kernel(
    tokens_hbm, cells_hbm, seam_hbm, obs_hbm, gain_hbm,
    w_q, w_k, w_v, w_o, w_g, w_u, w_d, w_r_hbm,
    out, logits,
    tokens, cells, seam, obs, gain, w_r, wqkv, wo, wg, wu, wd,
    x1, tok, normed, qkv, local, sx, sb, ra, rb, hot_t, ff, ffb, cx, cb, px, pr,
    w_sem, r_send, r_recv, x_send, x_recv, p_send, p_recv, t_send, t_recv, tx_send, tx_recv,
):
    me = lax.axis_index("round")
    m = lax.axis_index("mp")
    z, y, core = me // 16, lax.rem(me // 2, 8), lax.rem(me, 2)

    def z_of(k):
        return lax.rem(z + distance(k), 8) * 16

    columns = [
        lax.rem(y + d, 8) * 2 + (c if swap else 1 - c)
        for d in ORDER
        for swap, c in ((False, core), (True, core))
    ]

    def each_round(act):
        def turn(k, carry):
            plane = z_of(k)
            for column in columns:
                act(plane + column, k)
            return carry

        lax.fori_loop(0, 7, turn, 0)
        for column in columns[:15]:
            act(z * 16 + column, 7)

    def x_peer(k):
        return lax.rem(m + k, NX)

    def near_peer(k):
        return me + (1 - 2 * core) * (k % 2), x_peer(k // 2)

    def send_rounds(src, dst, slot):
        def act(to, turn):
            pltpu.make_async_remote_copy(
                src_ref=src(to),
                dst_ref=dst.at[me],
                send_sem=r_send.at[slot],
                recv_sem=r_recv.at[slot],
                device_id=(to, m),
                device_id_type=MESH,
            ).start()

        each_round(act)

    def wait_rounds(buffer, sem, slot):
        others = buffer.at[pl.ds(0, ROUNDS - 1)]
        pltpu.make_async_copy(others, others, sem.at[slot]).wait()

    def send_x(src, dst, slot):
        started = []
        for k in (2, 1, 3):
            to = x_peer(k)
            copy = pltpu.make_async_remote_copy(
                src_ref=src(to),
                dst_ref=dst,
                send_sem=x_send.at[slot, k],
                recv_sem=x_recv.at[slot, k],
                device_id=(me, to),
                device_id_type=MESH,
            )
            copy.start()
            started.append(copy)
        return started

    def finish(started):
        for copy in started:
            copy.wait()

    chunk = pl.ds(pl.multiple_of(m * 128, 128), 128)
    first = [
        pltpu.make_async_copy(cells_hbm, cells, w_sem.at[7]),
        pltpu.make_async_copy(tokens_hbm.at[:, chunk], tokens, w_sem.at[8]),
        pltpu.make_async_copy(seam_hbm, seam, w_sem.at[9]),
        pltpu.make_async_copy(obs_hbm, obs, w_sem.at[10]),
        pltpu.make_async_copy(gain_hbm, gain, w_sem.at[11]),
        pltpu.make_async_copy(w_r_hbm, w_r, w_sem.at[12]),
    ]
    barrier = pltpu.get_barrier_semaphore()

    def greet(to, turn):
        pl.semaphore_signal(barrier, inc=1, device_id=(to, m), device_id_type=MESH)

    each_round(greet)
    for k in range(2, 8):
        pl.semaphore_signal(
            barrier, inc=1, device_id=near_peer(k), device_id_type=MESH
        )

    for load in first:
        load.start()

    loads = [
        pltpu.make_async_copy(w_q, wqkv.at[:, pl.ds(0, HD)], w_sem.at[0]),
        pltpu.make_async_copy(w_k, wqkv.at[:, pl.ds(HD, HD)], w_sem.at[1]),
        pltpu.make_async_copy(w_v, wqkv.at[:, pl.ds(2 * HD, HD)], w_sem.at[2]),
        pltpu.make_async_copy(w_g, wg, w_sem.at[3]),
        pltpu.make_async_copy(w_u, wu, w_sem.at[4]),
        pltpu.make_async_copy(w_d, wd, w_sem.at[5]),
        pltpu.make_async_copy(w_o, wo.at[m], w_sem.at[6]),
    ]
    for load in loads:
        load.start()

    for load in first:
        load.wait()
    cell_row = cells[...].astype(F32)
    diagonal = iota((128, 128), 0) == iota((128, 128), 1)
    lanes = iota((128, 512), 1)
    for b in range(4):
        part = cell_row[:, b * 128 : b * 128 + 128]
        col = jnp.sum(jnp.where(diagonal, part, 0.0), axis=1, keepdims=True)
        picked = mm(hot(lanes == col.astype(jnp.int32)), tokens[...])
        x1[b * 32 : b * 32 + 32] = picked.astype(BF16).reshape(32, 4, 128)
    pl.semaphore_wait(barrier, ROUNDS - 1 + 6)

    def send_tokens(to, turn):
        pltpu.make_async_remote_copy(
            src_ref=x1.at[to],
            dst_ref=tok.at[m, me],
            send_sem=t_send,
            recv_sem=t_recv.at[turn],
            device_id=(to, m),
            device_id_type=MESH,
        ).start()

    for column in columns[:15]:
        send_tokens(z * 16 + column, 7)

    def token_turn(i, carry):
        plane = z_of(6 - i)
        for column in columns:
            send_tokens(plane + column, 6 - i)
        return carry

    lax.fori_loop(0, 7, token_turn, 0)
    tok[m, me] = x1[me]
    loads[6].wait()
    share_wo = send_x(lambda i: wo.at[m], wo.at[m], 0)

    own_pick = lanes == 4 * me + (iota((128, 512), 0) & 3)
    own_col = jnp.sum(jnp.where(own_pick, cell_row, 0.0), axis=1, keepdims=True)
    obs_all = jnp.concatenate(
        [obs[...].astype(F32), jnp.zeros((112, 512), F32)], axis=0
    ).astype(BF16)
    support = mm_nt(hot(lanes == own_col.astype(jnp.int32)), obs_all)
    divisor = jnp.sqrt(128.0 * mm_nt(jnp.ones((8, 512), BF16), obs_all))[0:1]

    s, o = iota((SLOTS, 128), 0), iota((SLOTS, 128), 1)
    both_rows = jnp.where((s & 1) == 0, seam[0:1], seam[1:2]).astype(F32)
    slot_col = jnp.sum(jnp.where(o == (s >> 1), both_rows, 0.0), axis=1, keepdims=True)
    empty = slot_col < 0.0
    hot_g = hot(iota((SLOTS, ROWS), 1) == slot_col.astype(jnp.int32))
    same = iota((SLOTS, SLOTS), 0) == iota((SLOTS, SLOTS), 1)
    slot_row = jnp.sum(jnp.where(same, slot_col, 0.0), axis=0, keepdims=True)
    hot_t[...] = hot(iota((ROWS, SLOTS), 0) == slot_row.astype(jnp.int32))

    gain_row = gain[...]
    for load in loads[:3]:
        load.wait()
    forwards = []
    for k in TURNS:
        from_z = lax.rem(z + 8 - ORDER[k], 8) * 16
        plane = tok.at[m, pl.ds(from_z, 16)]
        landed = plane if k < 7 else tok.at[m, pl.ds(0, 15)]
        pltpu.make_async_copy(landed, landed, t_recv.at[k]).wait()
        for i in (2, 1, 3):
            copy = pltpu.make_async_remote_copy(
                src_ref=plane,
                dst_ref=plane,
                send_sem=tx_send.at[k, i],
                recv_sem=tx_recv.at[k, i],
                device_id=(me, x_peer(i)),
                device_id_type=MESH,
            )
            copy.start()
            forwards.append(copy)
    for n, k in enumerate(TURNS):
        for copy in forwards[3 * n : 3 * n + 3]:
            copy.wait_recv()
        from_z = lax.rem(z + 8 - ORDER[k], 8)
        at = pl.ds(from_z * 16, 16)
        values = jnp.concatenate(
            [tok[i, at].reshape(64, 128) for i in range(NX)], axis=1
        ).astype(F32)
        spread = jnp.mean(values * values, axis=-1, keepdims=True)
        normal = (values * lax.rsqrt(spread + EPS) * gain_row).astype(BF16)
        normed[pl.ds(pl.multiple_of(from_z * 64, 64), 64), :] = normal
    qkv[...] = mm(normed[...], wqkv[...]).astype(BF16)

    sent = mm(hot_g, qkv[...])
    sent = jnp.where((iota((SLOTS, 3 * HD), 1) == 0) & empty, MARK, sent).astype(BF16)
    sx[...] = sent.reshape(ROUNDS, 2, 3 * HD)
    send_rounds(lambda i: sx.at[i], sb, 1)
    sb[me] = sx[me]

    for load in loads[3:6]:
        load.wait()

    def ff_step(i, carry):
        block = normed[pl.ds(pl.multiple_of(i * 128, 128), 128), :]
        gate = mm(block, wg[...])
        up = mm(block, wu[...])
        hidden = (gate * (1.0 / (1.0 + jnp.exp(-gate))) * up).astype(BF16)
        ff[i] = mm(hidden, wd[...])
        return carry

    lax.fori_loop(0, 4, ff_step, 0)
    share_ff = send_x(lambda i: ff.at[i], ffb.at[m], 1)
    ffb[m] = ff[m]

    low = iota((ROWS, HD), 1) < 64
    for h in range(2):
        half = low if h == 0 else jnp.logical_not(low)
        keys = jnp.where(half, qkv[:, HD : 2 * HD], 0.0).astype(BF16)
        values = jnp.where(half, qkv[:, 2 * HD : 3 * HD], 0.0).astype(BF16)
        for blk in range(2):
            at = slice(blk * 256, blk * 256 + 256)
            mix = mm(softmax(mm_nt(qkv[at, 0:HD], keys)), values)
            if h == 0:
                local[at, :] = mix
            else:
                local[at, :] += mix

    wait_rounds(sb, r_recv, 1)
    held = sb[...].reshape(SLOTS, 3 * HD)
    sq = held[:, 0:HD].astype(F32)
    sk, sv = held[:, HD : 2 * HD].astype(F32), held[:, 2 * HD :].astype(F32)
    dead = sq[:, 0:1] > 1e20
    sq = jnp.where(dead, 0.0, sq)
    lane = iota((SLOTS, HD), 1)
    total = jnp.zeros((SLOTS, HD), F32)
    for h in range(2):
        half = lane < 64 if h == 0 else lane >= 64
        spot = lane == (64 if h == 0 else 0)
        queries = jnp.where(half, sq, jnp.where(spot, 1.0, 0.0)).astype(BF16)
        keys = jnp.where(half, sk, jnp.where(spot & dead, DEAD, 0.0)).astype(BF16)
        values = jnp.where(half, sv, 0.0).astype(BF16)
        total += mm(softmax(mm_nt(queries, keys)), values)
    ra[...] = total.astype(BF16).reshape(ROUNDS, 2, HD)
    send_rounds(lambda i: ra.at[i], rb, 2)
    rb[me] = ra[me]

    own_tok = jnp.concatenate(
        [tok[i, pl.ds(m * 32, 32)].reshape(128, 128) for i in range(NX)], axis=1
    ).astype(F32)
    finish(share_ff)
    base = own_tok + (ffb[0] + ffb[1] + ffb[2] + ffb[3])
    wait_rounds(rb, r_recv, 2)

    both = local[...] + mm(hot_t[...], rb[...].reshape(SLOTS, HD))
    cx[...] = both.astype(BF16).reshape(NX, 128, HD)
    comb_x = send_x(lambda i: cx.at[i], cb.at[m], 2)
    cb[m] = cx[m]
    finish(comb_x)
    finish(share_wo)
    attn = mm(cb[0], wo[0]) + mm(cb[1], wo[1]) + mm(cb[2], wo[2]) + mm(cb[3], wo[3])
    result = (base + attn).astype(BF16)
    out[...] = result.reshape(32, 4, D)

    dots = jnp.sum(result.astype(F32) * w_r[...], axis=1, keepdims=True)
    px[2 * m + core] = jnp.sum(support * dots, axis=0, keepdims=True)
    sums = []
    for k in range(1, 8):
        copy = pltpu.make_async_remote_copy(
            src_ref=px.at[2 * m + core],
            dst_ref=px.at[2 * m + core],
            send_sem=p_send.at[k],
            recv_sem=p_recv.at[k],
            device_id=near_peer(k),
            device_id_type=MESH,
        )
        copy.start()
        sums.append(copy)
    finish(sums)
    chip = z * 8 + y
    pr[chip] = jnp.sum(px[...], axis=0)

    def send_sum(plane, column):
        pltpu.make_async_remote_copy(
            src_ref=pr.at[chip],
            dst_ref=pr.at[chip],
            send_sem=r_send.at[3],
            recv_sem=r_recv.at[3],
            device_id=(plane + column, m),
            device_id_type=MESH,
        ).start()

    same_core = columns[1::2]

    def sum_turn(k, carry):
        plane = z_of(k)
        for column in same_core:
            send_sum(plane, column)
        return carry

    lax.fori_loop(0, 7, sum_turn, 0)
    for column in same_core[:7]:
        send_sum(z * 16, column)
    others = pr.at[pl.ds(0, 63)]
    pltpu.make_async_copy(others, others, r_recv.at[3]).wait()
    pooled = jnp.sum(pr[...], axis=0)
    logits[...] = (pooled / divisor)[:, 0:16]
    for slot, buffer in ((1, sb), (2, rb)):
        wait_rounds(buffer, r_send, slot)
    sent_tokens = x1.at[pl.ds(0, ROUNDS - 1)]
    pltpu.make_async_copy(sent_tokens, sent_tokens, t_send).wait()
    pltpu.make_async_copy(others, others, r_send.at[3]).wait()
    for copy in forwards:
        copy.wait_send()


def in_hbm(array):
    return pltpu.with_memory_space_constraint(array, pltpu.HBM)


def shards(
    tokens, cell_order, seam_rows, obs_mask, norm_gain,
    w_query, w_key, w_value, w_out, w_gate, w_up, w_down, w_read,
):
    vmem = pl.BlockSpec(memory_space=pltpu.VMEM)
    hbm = pl.BlockSpec(memory_space=pltpu.HBM)
    dma = pltpu.SemaphoreType.DMA
    V = pltpu.VMEM
    out, logits = pl.pallas_call(
        kernel,
        out_shape=(
            jax.ShapeDtypeStruct((32, 4, D), BF16),
            jax.ShapeDtypeStruct((1, 16), F32),
        ),
        in_specs=[hbm] * 13,
        out_specs=(vmem, vmem),
        scratch_shapes=[
            V((D, 128), BF16), V((1, 512), jnp.int32), V((2, 128), jnp.int32),
            V((16, 512), jnp.int32), V((1, D), F32), V((1, D), F32),
            V((D, 3 * HD), BF16), V((NX, HD, D), BF16),
            V((D, D), BF16), V((D, D), BF16), V((D, D), BF16),
            V((ROUNDS, 4, 128), BF16), V((NX, ROUNDS, 4, 128), BF16), V((ROWS, D), BF16),
            V((ROWS, 3 * HD), BF16), V((ROWS, HD), F32),
            V((ROUNDS, 2, 3 * HD), BF16), V((ROUNDS, 2, 3 * HD), BF16),
            V((ROUNDS, 2, HD), BF16), V((ROUNDS, 2, HD), BF16),
            V((ROWS, SLOTS), BF16), V((NX, 128, D), F32), V((NX, 128, D), F32),
            V((NX, 128, HD), BF16), V((NX, 128, HD), BF16),
            V((8, 1, 128), F32), V((64, 1, 128), F32),
            dma((13,)), dma((4,)), dma((4,)), dma((3, NX)), dma((3, NX)),
            dma((8,)), dma((8,)),
            dma, dma((8,)), dma((8, NX)), dma((8, NX)),
        ],
        compiler_params=pltpu.CompilerParams(
            collective_id=0, has_side_effects=True, vmem_limit_bytes=40 * 2 ** 20
        ),
    )(
        *[
            in_hbm(array)
            for array in (
                tokens.reshape(512, D), cell_order.reshape(1, 512), seam_rows[0].T,
                obs_mask, norm_gain.reshape(1, D), w_query, w_key, w_value, w_out,
                w_gate, w_up, w_down, w_read.reshape(1, D),
            )
        ]
    )
    return out, logits.reshape(16)


def solution(mesh):
    return jax.shard_map(
        shards,
        mesh=mesh,
        in_specs=(
            P("round", None, None),
            P(),
            P("round", None, None),
            P(),
            P(),
            P(None, "mp"),
            P(None, "mp"),
            P(None, "mp"),
            P("mp", None),
            P(None, "mp"),
            P(None, "mp"),
            P("mp", None),
            P(),
        ),
        out_specs=(P("mp", "round", None), P()),
        check_vma=False,
    )
```

```python
import jax
import jax.numpy as jnp
from jax import lax
from jax.experimental import pallas as pl
from jax.experimental.pallas import tpu as pltpu
from jax.sharding import PartitionSpec as P

F32 = jnp.float32
BF16 = jnp.bfloat16
MESH = pl.DeviceIdType.MESH
EPS = 1e-6
TURNS = (7, 6, 5, 4, 3, 2, 1, 0)
ROUNDS, NX = 128, 4
ORDER = (4, 3, 5, 2, 6, 1, 7, 0)


def distance(k):
    return 4 + (1 - 2 * lax.rem(k, 2)) * ((k + 1) // 2)

D, HD, ROWS, SLOTS = 512, 128, 512, 256
MARK = 2.0 ** 100
DEAD = -1e30


def iota(shape, axis):
    return lax.broadcasted_iota(jnp.int32, shape, axis)


def hot(mask):
    return jnp.where(mask, 1.0, 0.0).astype(BF16)


def mm(a, b):
    return jnp.dot(a, b, preferred_element_type=F32)


def mm_nt(a, b):
    return lax.dot_general(a, b, (((1,), (1,)), ((), ())), preferred_element_type=F32)


def softmax(scores):
    top = jnp.max(scores, axis=-1, keepdims=True)
    weights = jnp.exp((scores - top) * 0.125)
    total = jnp.sum(weights, axis=-1, keepdims=True)
    return (weights * (1.0 / total)).astype(BF16)


def kernel(
    tokens_hbm, cells_hbm, seam_hbm, obs_hbm, gain_hbm,
    w_q, w_k, w_v, w_o, w_g, w_u, w_d, w_r_hbm,
    out, logits,
    tokens, cells, seam, obs, gain, w_r, wqkv, wo, wg, wu, wd,
    x1, tok, normed, qkv, local, sx, sb, ra, rb, hot_t, ff, ffb, cx, cb, px, pr,
    w_sem, r_send, r_recv, x_send, x_recv, p_send, p_recv, t_send, t_recv, tx_send, tx_recv,
):
    me = lax.axis_index("round")
    m = lax.axis_index("mp")
    z, y, core = me // 16, lax.rem(me // 2, 8), lax.rem(me, 2)

    def z_of(k):
        return lax.rem(z + distance(k), 8) * 16

    columns = [
        lax.rem(y + d, 8) * 2 + (c if swap else 1 - c)
        for d in ORDER
        for swap, c in ((False, core), (True, core))
    ]

    def each_round(act):
        def turn(k, carry):
            plane = z_of(k)
            for column in columns:
                act(plane + column, k)
            return carry

        lax.fori_loop(0, 7, turn, 0)
        for column in columns[:15]:
            act(z * 16 + column, 7)

    def x_peer(k):
        return lax.rem(m + k, NX)

    def near_peer(k):
        return me + (1 - 2 * core) * (k % 2), x_peer(k // 2)

    def send_rounds(src, dst, slot):
        def act(to, turn):
            pltpu.make_async_remote_copy(
                src_ref=src(to),
                dst_ref=dst.at[me],
                send_sem=r_send.at[slot],
                recv_sem=r_recv.at[slot],
                device_id=(to, m),
                device_id_type=MESH,
            ).start()

        each_round(act)

    def wait_rounds(buffer, sem, slot):
        others = buffer.at[pl.ds(0, ROUNDS - 1)]
        pltpu.make_async_copy(others, others, sem.at[slot]).wait()

    def send_x(src, dst, slot):
        started = []
        for k in (2, 1, 3):
            to = x_peer(k)
            copy = pltpu.make_async_remote_copy(
                src_ref=src(to),
                dst_ref=dst,
                send_sem=x_send.at[slot, k],
                recv_sem=x_recv.at[slot, k],
                device_id=(me, to),
                device_id_type=MESH,
            )
            copy.start()
            started.append(copy)
        return started

    def finish(started):
        for copy in started:
            copy.wait()

    chunk = pl.ds(pl.multiple_of(m * 128, 128), 128)
    first = [
        pltpu.make_async_copy(cells_hbm, cells, w_sem.at[7]),
        pltpu.make_async_copy(tokens_hbm.at[:, chunk], tokens, w_sem.at[8]),
        pltpu.make_async_copy(seam_hbm, seam, w_sem.at[9]),
        pltpu.make_async_copy(obs_hbm, obs, w_sem.at[10]),
        pltpu.make_async_copy(gain_hbm, gain, w_sem.at[11]),
        pltpu.make_async_copy(w_r_hbm, w_r, w_sem.at[12]),
    ]
    barrier = pltpu.get_barrier_semaphore()

    def greet(to, turn):
        pl.semaphore_signal(barrier, inc=1, device_id=(to, m), device_id_type=MESH)

    each_round(greet)
    for k in range(2, 8):
        pl.semaphore_signal(
            barrier, inc=1, device_id=near_peer(k), device_id_type=MESH
        )

    for load in first:
        load.start()

    loads = [
        pltpu.make_async_copy(w_q, wqkv.at[:, pl.ds(0, HD)], w_sem.at[0]),
        pltpu.make_async_copy(w_k, wqkv.at[:, pl.ds(HD, HD)], w_sem.at[1]),
        pltpu.make_async_copy(w_v, wqkv.at[:, pl.ds(2 * HD, HD)], w_sem.at[2]),
        pltpu.make_async_copy(w_g, wg, w_sem.at[3]),
        pltpu.make_async_copy(w_u, wu, w_sem.at[4]),
        pltpu.make_async_copy(w_d, wd, w_sem.at[5]),
        pltpu.make_async_copy(w_o, wo.at[m], w_sem.at[6]),
    ]
    for load in loads:
        load.start()

    for load in first:
        load.wait()
    cell_row = cells[...].astype(F32)
    diagonal = iota((128, 128), 0) == iota((128, 128), 1)
    lanes = iota((128, 512), 1)
    for b in range(4):
        part = cell_row[:, b * 128 : b * 128 + 128]
        col = jnp.sum(jnp.where(diagonal, part, 0.0), axis=1, keepdims=True)
        picked = mm(hot(lanes == col.astype(jnp.int32)), tokens[...])
        x1[b * 32 : b * 32 + 32] = picked.astype(BF16).reshape(32, 4, 128)
    pl.semaphore_wait(barrier, ROUNDS - 1 + 6)

    def send_tokens(to, turn):
        pltpu.make_async_remote_copy(
            src_ref=x1.at[to],
            dst_ref=tok.at[m, me],
            send_sem=t_send,
            recv_sem=t_recv.at[turn],
            device_id=(to, m),
            device_id_type=MESH,
        ).start()

    for column in columns[:15]:
        send_tokens(z * 16 + column, 7)

    def token_turn(i, carry):
        plane = z_of(6 - i)
        for column in columns:
            send_tokens(plane + column, 6 - i)
        return carry

    lax.fori_loop(0, 7, token_turn, 0)
    tok[m, me] = x1[me]
    loads[6].wait()
    share_wo = send_x(lambda i: wo.at[m], wo.at[m], 0)

    own_pick = lanes == 4 * me + (iota((128, 512), 0) & 3)
    own_col = jnp.sum(jnp.where(own_pick, cell_row, 0.0), axis=1, keepdims=True)
    obs_all = jnp.concatenate(
        [obs[...].astype(F32), jnp.zeros((112, 512), F32)], axis=0
    ).astype(BF16)
    support = mm_nt(hot(lanes == own_col.astype(jnp.int32)), obs_all)
    divisor = jnp.sqrt(128.0 * mm_nt(jnp.ones((8, 512), BF16), obs_all))[0:1]

    s, o = iota((SLOTS, 128), 0), iota((SLOTS, 128), 1)
    both_rows = jnp.where((s & 1) == 0, seam[0:1], seam[1:2]).astype(F32)
    slot_col = jnp.sum(jnp.where(o == (s >> 1), both_rows, 0.0), axis=1, keepdims=True)
    empty = slot_col < 0.0
    hot_g = hot(iota((SLOTS, ROWS), 1) == slot_col.astype(jnp.int32))
    same = iota((SLOTS, SLOTS), 0) == iota((SLOTS, SLOTS), 1)
    slot_row = jnp.sum(jnp.where(same, slot_col, 0.0), axis=0, keepdims=True)
    hot_t[...] = hot(iota((ROWS, SLOTS), 0) == slot_row.astype(jnp.int32))

    gain_row = gain[...]
    for load in loads[:3]:
        load.wait()
    forwards = []
    for k in TURNS:
        from_z = lax.rem(z + 8 - ORDER[k], 8) * 16
        plane = tok.at[m, pl.ds(from_z, 16)]
        landed = plane if k < 7 else tok.at[m, pl.ds(0, 15)]
        pltpu.make_async_copy(landed, landed, t_recv.at[k]).wait()
        for i in (2, 1, 3):
            copy = pltpu.make_async_remote_copy(
                src_ref=plane,
                dst_ref=plane,
                send_sem=tx_send.at[k, i],
                recv_sem=tx_recv.at[k, i],
                device_id=(me, x_peer(i)),
                device_id_type=MESH,
            )
            copy.start()
            forwards.append(copy)
    for n, k in enumerate(TURNS):
        for copy in forwards[3 * n : 3 * n + 3]:
            copy.wait_recv()
        from_z = lax.rem(z + 8 - ORDER[k], 8)
        at = pl.ds(from_z * 16, 16)
        values = jnp.concatenate(
            [tok[i, at].reshape(64, 128) for i in range(NX)], axis=1
        ).astype(F32)
        spread = jnp.mean(values * values, axis=-1, keepdims=True)
        normal = (values * lax.rsqrt(spread + EPS) * gain_row).astype(BF16)
        here = pl.ds(pl.multiple_of(from_z * 64, 64), 64)
        normed[here, :] = normal
        qkv[here, :] = mm(normal, wqkv[...]).astype(BF16)

    sent = mm(hot_g, qkv[...])
    sent = jnp.where((iota((SLOTS, 3 * HD), 1) == 0) & empty, MARK, sent).astype(BF16)
    sx[...] = sent.reshape(ROUNDS, 2, 3 * HD)
    send_rounds(lambda i: sx.at[i], sb, 1)
    sb[me] = sx[me]

    for load in loads[3:6]:
        load.wait()

    def ff_step(i, carry):
        block = normed[pl.ds(pl.multiple_of(i * 128, 128), 128), :]
        gate = mm(block, wg[...])
        up = mm(block, wu[...])
        hidden = (gate * (1.0 / (1.0 + jnp.exp(-gate))) * up).astype(BF16)
        ff[i] = mm(hidden, wd[...])
        return carry

    lax.fori_loop(0, 4, ff_step, 0)
    share_ff = send_x(lambda i: ff.at[i], ffb.at[m], 1)
    ffb[m] = ff[m]

    low = iota((ROWS, HD), 1) < 64
    for h in range(2):
        half = low if h == 0 else jnp.logical_not(low)
        keys = jnp.where(half, qkv[:, HD : 2 * HD], 0.0).astype(BF16)
        values = jnp.where(half, qkv[:, 2 * HD : 3 * HD], 0.0).astype(BF16)
        for blk in range(2):
            at = slice(blk * 256, blk * 256 + 256)
            mix = mm(softmax(mm_nt(qkv[at, 0:HD], keys)), values)
            if h == 0:
                local[at, :] = mix
            else:
                local[at, :] += mix

    wait_rounds(sb, r_recv, 1)
    held = sb[...].reshape(SLOTS, 3 * HD)
    sq = held[:, 0:HD].astype(F32)
    sk, sv = held[:, HD : 2 * HD].astype(F32), held[:, 2 * HD :].astype(F32)
    dead = sq[:, 0:1] > 1e20
    sq = jnp.where(dead, 0.0, sq)
    lane = iota((SLOTS, HD), 1)
    total = jnp.zeros((SLOTS, HD), F32)
    for h in range(2):
        half = lane < 64 if h == 0 else lane >= 64
        spot = lane == (64 if h == 0 else 0)
        queries = jnp.where(half, sq, jnp.where(spot, 1.0, 0.0)).astype(BF16)
        keys = jnp.where(half, sk, jnp.where(spot & dead, DEAD, 0.0)).astype(BF16)
        values = jnp.where(half, sv, 0.0).astype(BF16)
        total += mm(softmax(mm_nt(queries, keys)), values)
    ra[...] = total.astype(BF16).reshape(ROUNDS, 2, HD)
    send_rounds(lambda i: ra.at[i], rb, 2)
    rb[me] = ra[me]

    own_tok = jnp.concatenate(
        [tok[i, pl.ds(m * 32, 32)].reshape(128, 128) for i in range(NX)], axis=1
    ).astype(F32)
    finish(share_ff)
    base = own_tok + (ffb[0] + ffb[1] + ffb[2] + ffb[3])
    wait_rounds(rb, r_recv, 2)

    both = local[...] + mm(hot_t[...], rb[...].reshape(SLOTS, HD))
    cx[...] = both.astype(BF16).reshape(NX, 128, HD)
    comb_x = send_x(lambda i: cx.at[i], cb.at[m], 2)
    cb[m] = cx[m]
    finish(comb_x)
    finish(share_wo)
    attn = mm(cb[0], wo[0]) + mm(cb[1], wo[1]) + mm(cb[2], wo[2]) + mm(cb[3], wo[3])
    result = (base + attn).astype(BF16)
    out[...] = result.reshape(32, 4, D)

    dots = jnp.sum(result.astype(F32) * w_r[...], axis=1, keepdims=True)
    px[2 * m + core] = jnp.sum(support * dots, axis=0, keepdims=True)
    sums = []
    for k in (4, 5, 2, 3, 6, 7, 1):
        copy = pltpu.make_async_remote_copy(
            src_ref=px.at[2 * m + core],
            dst_ref=px.at[2 * m + core],
            send_sem=p_send.at[k],
            recv_sem=p_recv.at[k],
            device_id=near_peer(k),
            device_id_type=MESH,
        )
        copy.start()
        sums.append(copy)
    finish(sums)
    chip = z * 8 + y
    pr[chip] = jnp.sum(px[...], axis=0)

    def send_sum(plane, column):
        pltpu.make_async_remote_copy(
            src_ref=pr.at[chip],
            dst_ref=pr.at[chip],
            send_sem=r_send.at[3],
            recv_sem=r_recv.at[3],
            device_id=(plane + column, m),
            device_id_type=MESH,
        ).start()

    same_core = columns[1::2]

    def sum_turn(k, carry):
        plane = z_of(k)
        for column in same_core:
            send_sum(plane, column)
        return carry

    lax.fori_loop(0, 7, sum_turn, 0)
    for column in same_core[:7]:
        send_sum(z * 16, column)
    others = pr.at[pl.ds(0, 63)]
    pltpu.make_async_copy(others, others, r_recv.at[3]).wait()
    pooled = jnp.sum(pr[...], axis=0)
    logits[...] = (pooled / divisor)[:, 0:16]
    for slot, buffer in ((1, sb), (2, rb)):
        wait_rounds(buffer, r_send, slot)
    sent_tokens = x1.at[pl.ds(0, ROUNDS - 1)]
    pltpu.make_async_copy(sent_tokens, sent_tokens, t_send).wait()
    pltpu.make_async_copy(others, others, r_send.at[3]).wait()
    for copy in forwards:
        copy.wait_send()


def in_hbm(array):
    return pltpu.with_memory_space_constraint(array, pltpu.HBM)


def shards(
    tokens, cell_order, seam_rows, obs_mask, norm_gain,
    w_query, w_key, w_value, w_out, w_gate, w_up, w_down, w_read,
):
    vmem = pl.BlockSpec(memory_space=pltpu.VMEM)
    hbm = pl.BlockSpec(memory_space=pltpu.HBM)
    dma = pltpu.SemaphoreType.DMA
    V = pltpu.VMEM
    out, logits = pl.pallas_call(
        kernel,
        out_shape=(
            jax.ShapeDtypeStruct((32, 4, D), BF16),
            jax.ShapeDtypeStruct((1, 16), F32),
        ),
        in_specs=[hbm] * 13,
        out_specs=(vmem, vmem),
        scratch_shapes=[
            V((D, 128), BF16), V((1, 512), jnp.int32), V((2, 128), jnp.int32),
            V((16, 512), jnp.int32), V((1, D), F32), V((1, D), F32),
            V((D, 3 * HD), BF16), V((NX, HD, D), BF16),
            V((D, D), BF16), V((D, D), BF16), V((D, D), BF16),
            V((ROUNDS, 4, 128), BF16), V((NX, ROUNDS, 4, 128), BF16), V((ROWS, D), BF16),
            V((ROWS, 3 * HD), BF16), V((ROWS, HD), F32),
            V((ROUNDS, 2, 3 * HD), BF16), V((ROUNDS, 2, 3 * HD), BF16),
            V((ROUNDS, 2, HD), BF16), V((ROUNDS, 2, HD), BF16),
            V((ROWS, SLOTS), BF16), V((NX, 128, D), F32), V((NX, 128, D), F32),
            V((NX, 128, HD), BF16), V((NX, 128, HD), BF16),
            V((8, 1, 128), F32), V((64, 1, 128), F32),
            dma((13,)), dma((4,)), dma((4,)), dma((3, NX)), dma((3, NX)),
            dma((8,)), dma((8,)),
            dma, dma((8,)), dma((8, NX)), dma((8, NX)),
        ],
        compiler_params=pltpu.CompilerParams(
            collective_id=0, has_side_effects=True, vmem_limit_bytes=40 * 2 ** 20
        ),
    )(
        *[
            in_hbm(array)
            for array in (
                tokens.reshape(512, D), cell_order.reshape(1, 512), seam_rows[0].T,
                obs_mask, norm_gain.reshape(1, D), w_query, w_key, w_value, w_out,
                w_gate, w_up, w_down, w_read.reshape(1, D),
            )
        ]
    )
    return out, logits.reshape(16)


def solution(mesh):
    return jax.shard_map(
        shards,
        mesh=mesh,
        in_specs=(
            P("round", None, None),
            P(),
            P("round", None, None),
            P(),
            P(),
            P(None, "mp"),
            P(None, "mp"),
            P(None, "mp"),
            P("mp", None),
            P(None, "mp"),
            P(None, "mp"),
            P("mp", None),
            P(),
        ),
        out_specs=(P("mp", "round", None), P()),
        check_vma=False,
    )
```
